32 devices in a mesh: coil: 4 (over x, core), slab: 8 (over z, y).
Axes of the slice: x: 2, y: 2, z: 4, core: 2. Of those that a mesh axis runs over, the one named last changes fastest.
Arguments:
- kspace: bfloat16 [2, 8, 2, 32, 384, 128], P(None, 'coil', None, None, 'slab'), may hold values from -6 to 6
- coil_maps: bfloat16 [2, 8, 32, 384, 384], P(None, 'coil', None, 'slab'), may hold values from -1.1953125 to 1.1953125
- line_index: int32 [2, 384, 128], P(None, 'slab'), may hold values from 0 to 383, as said below
Outputs:
- harmonic_image: float32 [32, 2, 384, 384], P('coil', None, 'slab')
The draws below stay inside these ranges and needn't reach their ends.
Inputs may be any that keep to these rules, and one draw needn't show every extreme that they name: `line_index`: for each phase offset and kz plane the 128 ky indices are distinct.
All inputs are finite; a program needn't handle non-finite values.
Results may differ from the reference program's by a relative error of at most 0.0043.
Values may be sent and summed in bfloat16 or wider, within the bound.
A program may use at most 64 MiB of HBM per device.

```python
import math
import jax
import jax.numpy as jnp
from jax import lax

NY = 384
NZ = 384
LINES = 128
OFFS = 2
PHASES = 8
XR = 32
COILS = 8


def pick_row(row_key):
    return jax.random.permutation(row_key, NY)[:LINES]


def draw_line_index(key, part):
    row_keys = jax.random.split(jax.random.fold_in(key, 17), OFFS * NZ)
    chosen = jax.vmap(pick_row)(row_keys)
    return chosen.reshape(OFFS, NZ, LINES).astype(jnp.int32)


def raised(result, rng, source, target, shards_of, factor):
    def block_of(position):
        return (jnp.arange(result.shape[position]) // (result.shape[position] // shards_of)).reshape((-1,) + (1,) * (result.ndim - 1 - position))

    first = jax.random.permutation(rng, shards_of)[block_of(target)]
    second = (block_of(target) + shards_of // 2) % shards_of
    return jnp.where((block_of(source) == first) | (block_of(source) == second), factor * result, result)


def level_of(key, dims, shards, least, top_value):
    level = 1.0
    for axis_at, parts in shards:
        draws = jax.random.uniform(jax.random.fold_in(jax.random.fold_in(key, 6), axis_at), (parts,), jnp.float32, least / len(shards), top_value / len(shards))
        level = level * jnp.repeat(jnp.exp(draws), dims[axis_at] // parts).reshape((-1,) + (1,) * (len(dims) - 1 - axis_at))
    return level


def bell_draw(own_key, dims, scale, most, pieces=(), kind=jnp.bfloat16):
    array = scale * jax.random.normal(own_key, dims, jnp.float32)
    if pieces:
        array = array * level_of(own_key, dims, pieces, -0.22, 0.18)
    return jnp.clip(array, -most, most).astype(kind)


def heavy_noise(rng, shape, width, limit, pieces, heavy, dtype=jnp.bfloat16):
    values = width * jax.random.normal(rng, shape, jnp.float32)
    if pieces:
        values = values * level_of(rng, shape, pieces, -0.22, 0.18)
    return jnp.clip(raised(values, jax.random.fold_in(rng, 3), *heavy), -limit, limit).astype(dtype)


def setup_inputs(seed: int = 0) -> dict:
    arg_keys = jax.random.split(jax.random.key(seed), 4)
    return {
        "kspace": bell_draw(arg_keys[0], (2, COILS, OFFS, XR, NZ, LINES), 1.0, 6.0, ((1, 4), (4, 8))),
        "coil_maps": heavy_noise(arg_keys[1], (2, COILS, XR, NY, NZ), 0.2, 1.1953125, ((1, 4), (3, 8)), (1, 2, 4, 2.0)),
        "line_index": draw_line_index(jax.random.fold_in(arg_keys[3], 71), 0),
    }


def line_tables(line_index, length):
    positions = lax.broadcasted_iota(jnp.int32, (1, 1, 1, length), 3)
    turn_count = line_index[..., None] * positions % length
    angles = turn_count.astype(jnp.float32) * (2.0 * math.pi / length)
    scaling = 1.0 / math.sqrt(length)
    return ((jnp.cos(angles) * scaling).astype(jnp.bfloat16), (jnp.sin(angles) * scaling).astype(jnp.bfloat16))

def dense_tables(length):
    row_pos = lax.broadcasted_iota(jnp.int32, (length, length), 0)
    col_pos = lax.broadcasted_iota(jnp.int32, (length, length), 1)
    turn_count = row_pos * col_pos % length
    angles = turn_count.astype(jnp.float32) * (2.0 * math.pi / length)
    scaling = 1.0 / math.sqrt(length)
    return ((jnp.cos(angles) * scaling).astype(jnp.bfloat16), (jnp.sin(angles) * scaling).astype(jnp.bfloat16))

def fold_offsets(real_part, imag_part, fold_axis):
    sum_real = None
    sum_imag = None
    for offset in range(real_part.shape[fold_axis]):
        phase_angle = 2.0 * math.pi * offset / PHASES
        cosine = math.cos(phase_angle)
        sine = math.sin(phase_angle)
        here_real = jnp.take(real_part, offset, axis=fold_axis)
        here_imag = jnp.take(imag_part, offset, axis=fold_axis)
        term_real = cosine * here_real + sine * here_imag
        term_imag = cosine * here_imag - sine * here_real
        if sum_real is None:
            sum_real, sum_imag = (term_real, term_imag)
        else:
            sum_real, sum_imag = (sum_real + term_real, sum_imag + term_imag)
    return jnp.stack([sum_real, sum_imag]).astype(jnp.bfloat16)

def reference(kspace, coil_maps, line_index):
    line_cos, line_sin = line_tables(line_index, NY)
    line_cos = line_cos.astype(jnp.float32)
    line_sin = line_sin.astype(jnp.float32)
    depth_cos, depth_sin = dense_tables(NZ)
    depth_cos = depth_cos.astype(jnp.float32)
    depth_sin = depth_sin.astype(jnp.float32)
    highest = lax.Precision.HIGHEST

    def one_coil(coil, totals):
        samples = lax.dynamic_index_in_dim(kspace, coil, 1, keepdims=False).astype(jnp.float32)

        def lines_to_rows(left, right):
            return jnp.einsum('txkl,tkly->txyk', left, right, precision=highest)
        hybrid_real = lines_to_rows(samples[0], line_cos) - lines_to_rows(samples[1], line_sin)
        hybrid_imag = lines_to_rows(samples[0], line_sin) + lines_to_rows(samples[1], line_cos)
        folded = fold_offsets(hybrid_real, hybrid_imag, 0).astype(jnp.float32)

        def depth(left, right):
            return jnp.einsum('xyk,kz->xyz', left, right, precision=highest)
        image_real = depth(folded[0], depth_cos) - depth(folded[1], depth_sin)
        image_imag = depth(folded[0], depth_sin) + depth(folded[1], depth_cos)
        maps = lax.dynamic_index_in_dim(coil_maps, coil, 1, keepdims=False).astype(jnp.float32)
        add_real = maps[0] * image_real + maps[1] * image_imag
        add_imag = maps[0] * image_imag - maps[1] * image_real
        return (totals[0] + add_real, totals[1] + add_imag)
    zeros = jnp.zeros((XR, NY, NZ), jnp.float32)
    sum_real, sum_imag = lax.fori_loop(0, COILS, one_coil, (zeros, zeros))
    return jnp.stack([sum_real, sum_imag], axis=1)
```

```python
import functools
import math

import jax
import jax.numpy as jnp
import numpy as np
from jax import lax
from jax.experimental import pallas as pl
from jax.experimental.pallas import tpu as pltpu
from jax.sharding import PartitionSpec as P

PHASES = 8
LANES = 128
UNROLL = 8
VLIM = 52
ROWS = 16
MESH = pl.DeviceIdType.MESH


def across(me, slab):
    half = slab // 2
    other = half - lax.div(me, half) * half
    return [other + i for i in range(half)]


def beside(me, slab):
    half = slab // 2
    first = lax.div(me, half) * half
    return [first + lax.rem(me + i, half) for i in range(1, half)]


def up(value, unit):
    return -(-value // unit) * unit


def dense_table(rows, row_ok, length):
    turns = rows[:, None].astype(np.int64) * np.arange(length)[None, :] % length
    angles = turns.astype(np.float64) * (2.0 * math.pi / length)
    scaling = row_ok[:, None] / math.sqrt(length)
    cos, sin = np.cos(angles) * scaling, np.sin(angles) * scaling
    return np.concatenate([cos, sin], 1), np.concatenate([-sin, cos], 1)


def kernel(
    dims,
    kspace_ref, maps_ref, index_ref, ky_ref, kz_ref, out_ref,
    raw, index, samples, grid, maps, ky_tab, kz_tab, send, recv, image, part_send, part_recv,
    in_sem, load_sem, send_sem, recv_sem, last_sem, own_sem, psend_sem, precv_sem,
):
    slab, coil, coils, offs, xr, kzb, kzp, lines, ny, yb, nz = dims
    me_s, me_c = lax.axis_index("slab"), lax.axis_index("coil")
    rows = 2 * coils * slab
    kzs = up(kzb, 8)
    chunks = xr // slab
    last = chunks - 1
    xo = xr // coil
    owners = slab // xo
    blocks = kzp // ROWS

    barrier = pltpu.get_barrier_semaphore()
    for o in range(1, slab):
        pl.semaphore_signal(
            barrier, inc=1, device_id={"slab": lax.rem(me_s + o, slab)}, device_id_type=MESH
        )
    for o in range(1, coil):
        pl.semaphore_signal(
            barrier, inc=1, device_id={"coil": lax.rem(me_c + o, coil)}, device_id_type=MESH
        )

    def chunk_of(k):
        own = lax.div(me_c, owners)
        if chunks % 2:
            return lax.rem(own + 1 + k, chunks)
        pair = lax.rem(lax.div(own, 2) + 1 + lax.div(k, 2), chunks // 2)
        return 2 * pair + lax.rem(own + 1 + k, 2)

    count = min(ROWS, kzb)

    def load_k(k, b):
        at = pl.ds(chunk_of(k) * slab, slab)
        planes = pl.ds(b * ROWS, count)
        return pltpu.make_async_copy(
            kspace_ref.at[:, :, :, at, planes], raw.at[:, :, :, at, planes], load_sem.at[k, b]
        )

    load_i = pltpu.make_async_copy(index_ref, index, in_sem.at[3])
    load_m = pltpu.make_async_copy(maps_ref, maps, in_sem.at[0])
    load_y = pltpu.make_async_copy(ky_ref, ky_tab, in_sem.at[1])
    load_z = pltpu.make_async_copy(kz_ref, kz_tab, in_sem.at[2])
    load_k(jnp.int32(0), 0).start()
    load_i.start()
    load_y.start()

    if kzp != kzb:
        grid[...] = jnp.zeros_like(grid)

    def unpack(first, b, i, carry):
        kz_at = pl.multiple_of(b * ROWS, ROWS)
        for c in range(coils):
            for t in range(offs):
                angle = 2.0 * math.pi * t / PHASES
                real = raw[0, c, t, first + i, pl.ds(kz_at, count)].astype(jnp.float32)
                imag = raw[1, c, t, first + i, pl.ds(kz_at, count)].astype(jnp.float32)
                if t:
                    cosine, sine = math.cos(angle), math.sin(angle)
                    real, imag = cosine * real + sine * imag, cosine * imag - sine * real
                for part, value in ((0, real), (1, imag)):
                    at = pl.multiple_of(((part * coils + c) * slab + i) * kzs + kz_at, 8)
                    samples[t, pl.ds(at, count), :] = value
        return carry

    ky_at = lax.broadcasted_iota(jnp.int32, (ny, offs * lines), 0)

    def place(first_kz, step, carry):
        kz = first_kz + step
        picked = jnp.concatenate([index[t, pl.ds(kz, 1), :] for t in range(offs)], axis=1)
        hot = jnp.where(ky_at == picked, 1.0, 0.0).astype(jnp.bfloat16)
        left = jnp.concatenate(
            [samples[t, pl.ds(kz, rows, stride=kzs), :].astype(jnp.bfloat16) for t in range(offs)],
            axis=1,
        )
        grid_at = pl.multiple_of(kz * rows, 8)
        placed = lax.dot_general(
            left, hot, (((1,), (1,)), ((), ())), preferred_element_type=jnp.float32
        )
        for j in range(ny // LANES):
            grid[j, pl.ds(grid_at, rows), :] = placed[:, j * LANES : (j + 1) * LANES]
        return carry


    def block_copy(k, b, c, d, arrived):
        planes = pl.ds(pl.multiple_of(b * ROWS, ROWS), ROWS)
        return pltpu.make_async_remote_copy(
            src_ref=send.at[k, c, d, :, planes],
            dst_ref=recv.at[k, c, me_s, :, planes],
            send_sem=send_sem.at[k, c, d],
            recv_sem=arrived,
            device_id={"slab": d},
            device_id_type=MESH,
        )

    def whole_copy(k, c, d):
        return pltpu.make_async_remote_copy(
            src_ref=send.at[k, c, d],
            dst_ref=recv.at[k, c, d],
            send_sem=send_sem.at[k, c, d],
            recv_sem=recv_sem.at[k, c, d],
            device_id={"slab": d},
            device_id_type=MESH,
        )

    others = [lax.rem(me_s + o, slab) for o in range(1, slab)]

    def own_copy(k, c):
        return pltpu.make_async_copy(send.at[k, c, me_s], recv.at[k, c, me_s], own_sem.at[k, c])

    lane = lax.broadcasted_iota(jnp.int32, (ROWS, LANES), 1)

    def rows_pass(k, b, c, carry):
        kz_at = pl.multiple_of(b * ROWS, ROWS)
        lefts = []
        for i in range(slab):
            pieces = []
            for part in range(2):
                at = (part * coils + c) * slab + i
                for j in range(ny // LANES):
                    here = grid[j, pl.ds(kz_at * rows + at, ROWS, stride=rows), :]
                    pieces.append(here.astype(jnp.bfloat16))
            lefts.append(jnp.concatenate(pieces, axis=1))
        hybrid = jnp.dot(
            jnp.concatenate(lefts, axis=0), ky_tab[...], preferred_element_type=jnp.float32
        )
        for part in range(2):
            turned = []
            for i in range(slab):
                value = hybrid[i * ROWS : (i + 1) * ROWS, part * ny : (part + 1) * ny]
                turned.append(pltpu.roll(value, i * yb, 1) if i else value)
            for d in range(slab):
                for j in range(ny // LANES):
                    low, high = j * LANES // yb, ((j + 1) * LANES - 1) // yb
                    cut = slice(j * LANES, (j + 1) * LANES)
                    tile = turned[(low - d) % slab][:, cut]
                    for p in range(low + 1, high + 1):
                        tile = jnp.where(
                            lane >= p * yb - j * LANES, turned[(p - d) % slab][:, cut], tile
                        )
                    send[k, c, d, part, pl.ds(kz_at, ROWS), cut] = tile.astype(jnp.bfloat16)

        @pl.when((k == 0) & (b == 0) & (c == 0))
        def _():
            pl.semaphore_wait(barrier, slab + coil - 2)

        @pl.when(k < last)
        def _():
            for d in across(me_s, slab) + beside(me_s, slab):
                block_copy(k, b, c, d, recv_sem.at[k, c, me_s]).start()

        @pl.when(b == blocks - 1)
        def _():
            own_copy(k, c).start()

        return carry

    def chunk_pass(k, carry):
        first = chunk_of(k) * slab

        def block_pass(b, inner):
            load_k(k, b).wait()
            lax.fori_loop(0, slab, functools.partial(unpack, first, b), 0)
            lax.fori_loop(0, count, functools.partial(place, b * ROWS), 0, unroll=UNROLL)
            lax.fori_loop(0, coils, functools.partial(rows_pass, k, b), 0)

            @pl.when((k == 0) & (b == 0))
            def _():
                for j in range(1, chunks * blocks):
                    load_k(jnp.int32(j // blocks), j % blocks).start()
                load_m.start()
                load_z.start()

            return inner

        return lax.fori_loop(0, blocks, block_pass, carry)

    load_i.wait()
    load_y.wait()
    lax.fori_loop(0, chunks, chunk_pass, 0)
    for d in beside(me_s, slab) + across(me_s, slab):
        for b in range(blocks):
            for c in range(coils):
                block_copy(last, b, c, d, last_sem.at[b, c, me_s]).start()
    load_m.wait()
    load_z.wait()

    def part_copy(k, q):
        owner = chunk_of(k) * owners + q
        return pltpu.make_async_remote_copy(
            src_ref=part_send.at[chunk_of(k), pl.ds(q * xo, xo)],
            dst_ref=part_recv.at[lax.rem(owner - me_c + coil, coil)],
            send_sem=psend_sem.at[k, q],
            recv_sem=precv_sem.at[lax.rem(owner - me_c + coil, coil)],
            device_id={"coil": owner},
            device_id_type=MESH,
        )

    def depth(k, c, at, planes):
        block = recv[k, c, :, :, pl.ds(at, planes)].reshape(slab * 2 * planes, slab * yb)
        table = kz_tab[:, :, pl.ds(at, planes)].reshape(slab * 2 * planes, 2 * nz)
        return lax.dot_general(
            block, table, (((0,), (0,)), ((), ())), preferred_element_type=jnp.float32
        )

    def combined(c, p, x):
        real = image[c, pl.ds(p * yb, yb), :nz]
        imag = image[c, pl.ds(p * yb, yb), nz:]
        map_real = maps[0, c, x].astype(jnp.float32)
        map_imag = maps[1, c, x].astype(jnp.float32)
        return map_real * real + map_imag * imag, map_real * imag - map_imag * real

    def depth_pass(k, carry):
        first = chunk_of(k) * slab

        def one_coil(c, inner):
            own_copy(k, c).wait()
            @pl.when(k < last)
            def _():
                for d in others:
                    whole_copy(k, c, d).wait_recv()

            image[c] = depth(k, c, 0, kzp)
            return inner

        lax.fori_loop(0, coils, one_coil, 0)
        for p in range(slab):
            x = lax.rem(p - me_s + slab, slab)
            add_real, add_imag = combined(0, p, first + x)
            for c in range(1, coils):
                term_real, term_imag = combined(c, p, first + x)
                add_real, add_imag = add_real + term_real, add_imag + term_imag
            part_send[chunk_of(k), x, 0] = add_real.astype(jnp.bfloat16)
            part_send[chunk_of(k), x, 1] = add_imag.astype(jnp.bfloat16)
        for q in range(owners):
            @pl.when(chunk_of(k) * owners + q != me_c)
            def _():
                part_copy(k, q).start()
        return carry

    def wait_parts():
        for o in range(1, coil):
            pltpu.make_async_remote_copy(
                src_ref=part_recv.at[o],
                dst_ref=part_recv.at[o],
                send_sem=psend_sem.at[0, 0],
                recv_sem=precv_sem.at[o],
                device_id={"coil": lax.rem(me_c + o, coil)},
                device_id_type=MESH,
            ).wait_recv()

    def drain(k, carry):
        for c in range(coils):
            for d in others:
                whole_copy(k, c, d).wait_send()
        for q in range(owners):
            @pl.when(chunk_of(k) * owners + q != me_c)
            def _():
                part_copy(k, q).wait_send()
        return carry

    own_chunk = lax.div(me_c, owners)

    if owners == 1 and coil > 1:
        lax.fori_loop(0, last, depth_pass, 0)
        wait_parts()

        def total(i, carry):
            value = part_recv[1, i].astype(jnp.float32)
            for o in range(2, coil):
                value = value + part_recv[o, i].astype(jnp.float32)
            out_ref[i] = value
            return carry

        lax.fori_loop(0, xo, total, 0)
        for c in range(coils):
            own_copy(last, c).wait()

        def last_pass(j, carry):
            b, c = lax.div(j, coils), lax.rem(j, coils)

            @pl.when(j == blocks * coils - 1)
            def _():
                lax.fori_loop(0, last, drain, 0)

            for d in others:
                block_copy(last, b, c, d, last_sem.at[b, c, d]).wait_recv()
            image[c] = depth(last, c, pl.multiple_of(b * ROWS, ROWS), ROWS)
            for p in range(slab):
                x = lax.rem(p - me_s + slab, slab)
                add_real, add_imag = combined(c, p, own_chunk * slab + x)
                out_ref[x, 0] += add_real
                out_ref[x, 1] += add_imag
            return carry

        lax.fori_loop(0, blocks * coils, last_pass, 0)
        drain(last, 0)
    else:

        def gather(j, carry):
            b, c = lax.div(j, coils), lax.rem(j, coils)
            for d in others:
                block_copy(last, b, c, d, last_sem.at[b, c, d]).wait_recv()
            return carry

        lax.fori_loop(0, last, depth_pass, 0)
        lax.fori_loop(0, blocks * coils, gather, 0)
        depth_pass(last, 0)
        wait_parts()
        own_at = lax.rem(me_c, owners) * xo

        def total(i, carry):
            value = part_send[own_chunk, own_at + i].astype(jnp.float32)
            for o in range(1, coil):
                value = value + part_recv[o, i].astype(jnp.float32)
            out_ref[i] = value
            return carry

        lax.fori_loop(0, xo, total, 0)
        lax.fori_loop(0, chunks, drain, 0)


def local(mesh, kspace, coil_maps, line_index):
    slab, coil = mesh.shape["slab"], mesh.shape["coil"]
    _, coils, offs, xr, kzb, lines = kspace.shape
    yb, nz = coil_maps.shape[3:]
    ny = yb * slab
    kzp = up(kzb, 16)
    dims = (slab, coil, coils, offs, xr, kzb, kzp, lines, ny, yb, nz)
    chunks, xo = xr // slab, xr // coil
    owners = slab // xo
    rows = 2 * coils * slab
    f32, bf16 = jnp.float32, jnp.bfloat16

    ky_table = np.concatenate(dense_table(np.arange(ny), np.ones(ny), ny), 0)
    local_kz = np.arange(kzp)
    per_slab = []
    for s in range(slab):
        per_slab += dense_table(s * kzb + local_kz, (local_kz < kzb) * 1.0, nz)
    kz_table = np.concatenate(per_slab, 0).reshape(slab, 2, kzp, 2 * nz)
    ky_table = jnp.asarray(ky_table.astype(np.float32)).astype(bf16)
    kz_table = jnp.asarray(kz_table.astype(np.float32)).astype(bf16)

    vmem, hbm = pl.BlockSpec(memory_space=pltpu.VMEM), pl.BlockSpec(memory_space=pltpu.HBM)
    dma = pltpu.SemaphoreType.DMA
    return pl.pallas_call(
        functools.partial(kernel, dims),
        out_shape=jax.ShapeDtypeStruct((xo, 2, yb, nz), f32),
        in_specs=[hbm] * 5,
        out_specs=vmem,
        scratch_shapes=[
            pltpu.VMEM(kspace.shape, bf16),
            pltpu.VMEM(line_index.shape, jnp.int32),
            pltpu.VMEM((offs, rows * up(kzb, 8), lines), f32),
            pltpu.VMEM((ny // LANES, kzp * rows, LANES), f32),
            pltpu.VMEM(coil_maps.shape, bf16),
            pltpu.VMEM(ky_table.shape, bf16),
            pltpu.VMEM(kz_table.shape, bf16),
            pltpu.VMEM((chunks, coils, slab, 2, kzp, ny), bf16),
            pltpu.VMEM((chunks, coils, slab, 2, kzp, ny), bf16),
            pltpu.VMEM((coils, ny, 2 * nz), f32),
            pltpu.VMEM((chunks, slab, 2, yb, nz), bf16),
            pltpu.VMEM((coil, xo, 2, yb, nz), bf16),
            dma((4,)),
            dma((chunks, kzp // ROWS)),
            dma((chunks, coils, slab)),
            dma((chunks, coils, slab)),
            dma((kzp // ROWS, coils, slab)),
            dma((chunks, coils)),
            dma((chunks, owners)),
            dma((coil,)),
        ],
        compiler_params=pltpu.CompilerParams(
            collective_id=0, has_side_effects=True, vmem_limit_bytes=VLIM * 1024 * 1024
        ),
    )(kspace, coil_maps, line_index, ky_table, kz_table)


def solution(mesh):
    placed = (
        P(None, "coil", None, None, "slab", None),
        P(None, "coil", None, "slab", None),
        P(None, "slab", None),
    )
    return jax.shard_map(
        functools.partial(local, mesh),
        mesh=mesh,
        in_specs=placed,
        out_specs=P("coil", None, "slab", None),
        check_vma=False,
    )
```

```python
import functools
import math

import jax
import jax.numpy as jnp
import numpy as np
from jax import lax
from jax.experimental import pallas as pl
from jax.experimental.pallas import tpu as pltpu
from jax.sharding import PartitionSpec as P

PHASES = 8
LANES = 128
UNROLL = 8
VLIM = 52
ROWS = 16
MESH = pl.DeviceIdType.MESH


def across(me, slab):
    half = slab // 2
    other = half - lax.div(me, half) * half
    return [other + i for i in range(half)]


def beside(me, slab):
    half = slab // 2
    first = lax.div(me, half) * half
    return [first + lax.rem(me + i, half) for i in range(1, half)]


def up(value, unit):
    return -(-value // unit) * unit


def dense_table(rows, row_ok, length):
    turns = rows[:, None].astype(np.int64) * np.arange(length)[None, :] % length
    angles = turns.astype(np.float64) * (2.0 * math.pi / length)
    scaling = row_ok[:, None] / math.sqrt(length)
    cos, sin = np.cos(angles) * scaling, np.sin(angles) * scaling
    return np.concatenate([cos, sin], 1), np.concatenate([-sin, cos], 1)


def kernel(
    dims,
    kspace_ref, maps_ref, index_ref, ky_ref, kz_ref, out_ref,
    raw, index, samples, grid, maps, ky_tab, kz_tab, send, recv, image, part_send, part_recv,
    in_sem, load_sem, send_sem, recv_sem, last_sem, own_sem, psend_sem, precv_sem,
):
    slab, coil, coils, offs, xr, kzb, kzp, lines, ny, yb, nz = dims
    me_s, me_c = lax.axis_index("slab"), lax.axis_index("coil")
    rows = 2 * coils * slab
    kzs = up(kzb, 8)
    chunks = xr // slab
    last = chunks - 1
    xo = xr // coil
    owners = slab // xo
    blocks = kzp // ROWS
    early = (blocks - 1) * ROWS

    def chunk_of(k):
        own = lax.div(me_c, owners)
        if chunks % 2:
            return lax.rem(own + 1 + k, chunks)
        pair = lax.rem(lax.div(own, 2) + 1 + lax.div(k, 2), chunks // 2)
        return 2 * pair + lax.rem(own + 1 + k, 2)

    count = min(ROWS, kzb)

    def load_k(k, b):
        at = pl.ds(chunk_of(k) * slab, slab)
        planes = pl.ds(b * ROWS, count)
        return pltpu.make_async_copy(
            kspace_ref.at[:, :, :, at, planes], raw.at[:, :, :, at, planes], load_sem.at[k, b]
        )

    load_i = pltpu.make_async_copy(index_ref, index, in_sem.at[3])
    load_m = pltpu.make_async_copy(maps_ref, maps, in_sem.at[0])
    load_y = pltpu.make_async_copy(ky_ref, ky_tab, in_sem.at[1])
    load_z = pltpu.make_async_copy(kz_ref, kz_tab, in_sem.at[2])
    load_k(jnp.int32(0), 0).start()
    load_i.start()
    load_y.start()

    barrier = pltpu.get_barrier_semaphore()
    for o in range(1, slab):
        pl.semaphore_signal(
            barrier, inc=1, device_id={"slab": lax.rem(me_s + o, slab)}, device_id_type=MESH
        )
    for o in range(1, coil):
        pl.semaphore_signal(
            barrier, inc=1, device_id={"coil": lax.rem(me_c + o, coil)}, device_id_type=MESH
        )

    if kzp != kzb:
        grid[...] = jnp.zeros_like(grid)

    def unpack(first, b, i, carry):
        kz_at = pl.multiple_of(b * ROWS, ROWS)
        for c in range(coils):
            for t in range(offs):
                angle = 2.0 * math.pi * t / PHASES
                real = raw[0, c, t, first + i, pl.ds(kz_at, count)].astype(jnp.float32)
                imag = raw[1, c, t, first + i, pl.ds(kz_at, count)].astype(jnp.float32)
                if t:
                    cosine, sine = math.cos(angle), math.sin(angle)
                    real, imag = cosine * real + sine * imag, cosine * imag - sine * real
                for part, value in ((0, real), (1, imag)):
                    at = pl.multiple_of(((part * coils + c) * slab + i) * kzs + kz_at, 8)
                    samples[t, pl.ds(at, count), :] = value
        return carry

    ky_at = lax.broadcasted_iota(jnp.int32, (ny, offs * lines), 0)

    def place(first_kz, step, carry):
        kz = first_kz + step
        picked = jnp.concatenate([index[t, pl.ds(kz, 1), :] for t in range(offs)], axis=1)
        hot = jnp.where(ky_at == picked, 1.0, 0.0).astype(jnp.bfloat16)
        left = jnp.concatenate(
            [samples[t, pl.ds(kz, rows, stride=kzs), :].astype(jnp.bfloat16) for t in range(offs)],
            axis=1,
        )
        grid_at = pl.multiple_of(kz * rows, 8)
        placed = lax.dot_general(
            left, hot, (((1,), (1,)), ((), ())), preferred_element_type=jnp.float32
        )
        for j in range(ny // LANES):
            grid[j, pl.ds(grid_at, rows), :] = placed[:, j * LANES : (j + 1) * LANES]
        return carry


    def block_copy(k, b, c, d, arrived):
        planes = pl.ds(pl.multiple_of(b * ROWS, ROWS), ROWS)
        return pltpu.make_async_remote_copy(
            src_ref=send.at[k, c, d, :, planes],
            dst_ref=recv.at[k, c, me_s, :, planes],
            send_sem=send_sem.at[k],
            recv_sem=arrived,
            device_id={"slab": d},
            device_id_type=MESH,
        )

    def all_of(k, c, planes, arrived):
        return pltpu.make_async_remote_copy(
            src_ref=recv.at[k, c, pl.ds(0, slab - 1), :, planes],
            dst_ref=recv.at[k, c, pl.ds(0, slab - 1), :, planes],
            send_sem=send_sem.at[k],
            recv_sem=arrived,
            device_id={"slab": lax.rem(me_s + 1, slab)},
            device_id_type=MESH,
        )

    def all_sent(k):
        return pltpu.make_async_remote_copy(
            src_ref=send.at[k, :, pl.ds(0, slab - 1)],
            dst_ref=recv.at[k, :, pl.ds(0, slab - 1)],
            send_sem=send_sem.at[k],
            recv_sem=recv_sem.at[k, 0],
            device_id={"slab": lax.rem(me_s + 1, slab)},
            device_id_type=MESH,
        )

    def own_copy(k, c):
        return pltpu.make_async_copy(send.at[k, c, me_s], recv.at[k, c, me_s], own_sem.at[k, c])

    lane = lax.broadcasted_iota(jnp.int32, (ROWS, LANES), 1)

    def rows_pass(k, b, c, carry):
        kz_at = pl.multiple_of(b * ROWS, ROWS)
        lefts = []
        for i in range(slab):
            pieces = []
            for part in range(2):
                at = (part * coils + c) * slab + i
                for j in range(ny // LANES):
                    here = grid[j, pl.ds(kz_at * rows + at, ROWS, stride=rows), :]
                    pieces.append(here.astype(jnp.bfloat16))
            lefts.append(jnp.concatenate(pieces, axis=1))
        hybrid = jnp.dot(
            jnp.concatenate(lefts, axis=0), ky_tab[...], preferred_element_type=jnp.float32
        )
        for part in range(2):
            turned = []
            for i in range(slab):
                value = hybrid[i * ROWS : (i + 1) * ROWS, part * ny : (part + 1) * ny]
                turned.append(pltpu.roll(value, i * yb, 1) if i else value)
            for d in range(slab):
                for j in range(ny // LANES):
                    low, high = j * LANES // yb, ((j + 1) * LANES - 1) // yb
                    cut = slice(j * LANES, (j + 1) * LANES)
                    tile = turned[(low - d) % slab][:, cut]
                    for p in range(low + 1, high + 1):
                        tile = jnp.where(
                            lane >= p * yb - j * LANES, turned[(p - d) % slab][:, cut], tile
                        )
                    send[k, c, d, part, pl.ds(kz_at, ROWS), cut] = tile.astype(jnp.bfloat16)

        @pl.when((k == 0) & (b == 0) & (c == 0))
        def _():
            pl.semaphore_wait(barrier, slab + coil - 2)

        @pl.when((k < last) | (b < blocks - 1))
        def _():
            for d in across(me_s, slab) + beside(me_s, slab):
                block_copy(k, b, c, d, recv_sem.at[k, c]).start()

        @pl.when(b == blocks - 1)
        def _():
            own_copy(k, c).start()

        return carry

    def chunk_pass(k, carry):
        first = chunk_of(k) * slab

        def block_pass(b, inner):
            load_k(k, b).wait()
            lax.fori_loop(0, slab, functools.partial(unpack, first, b), 0)
            lax.fori_loop(0, count, functools.partial(place, b * ROWS), 0, unroll=UNROLL)

            @pl.when((k == 0) & (b == 0))
            def _():
                load_y.wait()

            lax.fori_loop(0, coils, functools.partial(rows_pass, k, b), 0)

            @pl.when((k == 0) & (b == 0))
            def _():
                for j in range(1, chunks * blocks):
                    load_k(jnp.int32(j // blocks), j % blocks).start()
                load_m.start()
                load_z.start()

            return inner

        return lax.fori_loop(0, blocks, block_pass, carry)

    load_i.wait()
    lax.fori_loop(0, chunks, chunk_pass, 0)
    for d in beside(me_s, slab) + across(me_s, slab):
        for c in range(coils):
            block_copy(last, blocks - 1, c, d, last_sem.at[c]).start()
    load_m.wait()
    load_z.wait()

    def part_copy(k, q):
        owner = chunk_of(k) * owners + q
        return pltpu.make_async_remote_copy(
            src_ref=part_send.at[chunk_of(k), pl.ds(q * xo, xo)],
            dst_ref=part_recv.at[lax.rem(owner - me_c + coil, coil)],
            send_sem=psend_sem.at[k, q],
            recv_sem=precv_sem.at[lax.rem(owner - me_c + coil, coil)],
            device_id={"coil": owner},
            device_id_type=MESH,
        )

    def depth(k, c, at, planes):
        block = recv[k, c, :, :, pl.ds(at, planes)].reshape(slab * 2 * planes, slab * yb)
        table = kz_tab[:, :, pl.ds(at, planes)].reshape(slab * 2 * planes, 2 * nz)
        return lax.dot_general(
            block, table, (((0,), (0,)), ((), ())), preferred_element_type=jnp.float32
        )

    def combined(c, p, x):
        real = image[c, pl.ds(p * yb, yb), :nz]
        imag = image[c, pl.ds(p * yb, yb), nz:]
        map_real = maps[0, c, x].astype(jnp.float32)
        map_imag = maps[1, c, x].astype(jnp.float32)
        return map_real * real + map_imag * imag, map_real * imag - map_imag * real

    def depth_pass(k, carry):
        first = chunk_of(k) * slab

        def one_coil(c, inner):
            own_copy(k, c).wait()
            @pl.when(k < last)
            def _():
                all_of(k, c, pl.ds(0, kzp), recv_sem.at[k, c]).wait_recv()

            image[c] = depth(k, c, 0, kzp)
            return inner

        lax.fori_loop(0, coils, one_coil, 0)
        for p in range(slab):
            x = lax.rem(p - me_s + slab, slab)
            add_real, add_imag = combined(0, p, first + x)
            for c in range(1, coils):
                term_real, term_imag = combined(c, p, first + x)
                add_real, add_imag = add_real + term_real, add_imag + term_imag
            part_send[chunk_of(k), x, 0] = add_real.astype(jnp.bfloat16)
            part_send[chunk_of(k), x, 1] = add_imag.astype(jnp.bfloat16)
        for q in range(owners):
            @pl.when(chunk_of(k) * owners + q != me_c)
            def _():
                part_copy(k, q).start()
        return carry

    def wait_parts():
        for o in range(1, coil):
            pltpu.make_async_remote_copy(
                src_ref=part_recv.at[o],
                dst_ref=part_recv.at[o],
                send_sem=psend_sem.at[0, 0],
                recv_sem=precv_sem.at[o],
                device_id={"coil": lax.rem(me_c + o, coil)},
                device_id_type=MESH,
            ).wait_recv()

    def drain(k, carry):
        all_sent(k).wait_send()
        for q in range(owners):
            @pl.when(chunk_of(k) * owners + q != me_c)
            def _():
                part_copy(k, q).wait_send()
        return carry

    own_chunk = lax.div(me_c, owners)

    if owners == 1 and coil > 1:
        lax.fori_loop(0, last, depth_pass, 0)
        wait_parts()

        def add_up(c):
            for p in range(slab):
                x = lax.rem(p - me_s + slab, slab)
                add_real, add_imag = combined(c, p, own_chunk * slab + x)
                out_ref[x, 0] += add_real
                out_ref[x, 1] += add_imag

        def total(i, carry):
            value = part_recv[1, i].astype(jnp.float32)
            for o in range(2, coil):
                value = value + part_recv[o, i].astype(jnp.float32)
            out_ref[i] = value
            return carry

        lax.fori_loop(0, xo, total, 0)
        for c in range(coils):
            own_copy(last, c).wait()
        if blocks > 1:
            for c in range(coils):
                all_of(last, c, pl.ds(0, early), recv_sem.at[last, c]).wait_recv()
                image[c] = depth(last, c, 0, early)
            for c in range(coils):
                add_up(c)
        lax.fori_loop(0, last, drain, 0)
        for c in range(coils):
            all_of(last, c, pl.ds(early, ROWS), last_sem.at[c]).wait_recv()
            image[c] = depth(last, c, early, ROWS)
            add_up(c)
        drain(last, 0)
    else:

        lax.fori_loop(0, last, depth_pass, 0)
        for c in range(coils):
            if blocks > 1:
                all_of(last, c, pl.ds(0, early), recv_sem.at[last, c]).wait_recv()
            all_of(last, c, pl.ds(early, ROWS), last_sem.at[c]).wait_recv()
        depth_pass(last, 0)
        wait_parts()
        own_at = lax.rem(me_c, owners) * xo

        def total(i, carry):
            value = part_send[own_chunk, own_at + i].astype(jnp.float32)
            for o in range(1, coil):
                value = value + part_recv[o, i].astype(jnp.float32)
            out_ref[i] = value
            return carry

        lax.fori_loop(0, xo, total, 0)
        lax.fori_loop(0, chunks, drain, 0)


def local(mesh, kspace, coil_maps, line_index):
    slab, coil = mesh.shape["slab"], mesh.shape["coil"]
    _, coils, offs, xr, kzb, lines = kspace.shape
    yb, nz = coil_maps.shape[3:]
    ny = yb * slab
    kzp = up(kzb, 16)
    dims = (slab, coil, coils, offs, xr, kzb, kzp, lines, ny, yb, nz)
    chunks, xo = xr // slab, xr // coil
    owners = slab // xo
    rows = 2 * coils * slab
    f32, bf16 = jnp.float32, jnp.bfloat16

    ky_table = np.concatenate(dense_table(np.arange(ny), np.ones(ny), ny), 0)
    local_kz = np.arange(kzp)
    per_slab = []
    for s in range(slab):
        per_slab += dense_table(s * kzb + local_kz, (local_kz < kzb) * 1.0, nz)
    kz_table = np.concatenate(per_slab, 0).reshape(slab, 2, kzp, 2 * nz)
    ky_table = jnp.asarray(ky_table.astype(np.float32)).astype(bf16)
    kz_table = jnp.asarray(kz_table.astype(np.float32)).astype(bf16)

    vmem, hbm = pl.BlockSpec(memory_space=pltpu.VMEM), pl.BlockSpec(memory_space=pltpu.HBM)
    dma = pltpu.SemaphoreType.DMA
    return pl.pallas_call(
        functools.partial(kernel, dims),
        out_shape=jax.ShapeDtypeStruct((xo, 2, yb, nz), f32),
        in_specs=[hbm] * 5,
        out_specs=vmem,
        scratch_shapes=[
            pltpu.VMEM(kspace.shape, bf16),
            pltpu.VMEM(line_index.shape, jnp.int32),
            pltpu.VMEM((offs, rows * up(kzb, 8), lines), f32),
            pltpu.VMEM((ny // LANES, kzp * rows, LANES), f32),
            pltpu.VMEM(coil_maps.shape, bf16),
            pltpu.VMEM(ky_table.shape, bf16),
            pltpu.VMEM(kz_table.shape, bf16),
            pltpu.VMEM((chunks, coils, slab, 2, kzp, ny), bf16),
            pltpu.VMEM((chunks, coils, slab, 2, kzp, ny), bf16),
            pltpu.VMEM((coils, ny, 2 * nz), f32),
            pltpu.VMEM((chunks, slab, 2, yb, nz), bf16),
            pltpu.VMEM((coil, xo, 2, yb, nz), bf16),
            dma((4,)),
            dma((chunks, kzp // ROWS)),
            dma((chunks,)),
            dma((chunks, coils)),
            dma((coils,)),
            dma((chunks, coils)),
            dma((chunks, owners)),
            dma((coil,)),
        ],
        compiler_params=pltpu.CompilerParams(
            collective_id=0, has_side_effects=True, vmem_limit_bytes=VLIM * 1024 * 1024
        ),
    )(kspace, coil_maps, pltpu.with_memory_space_constraint(line_index, pltpu.HBM), ky_table, kz_table)


def solution(mesh):
    placed = (
        P(None, "coil", None, None, "slab", None),
        P(None, "coil", None, "slab", None),
        P(None, "slab", None),
    )
    return jax.shard_map(
        functools.partial(local, mesh),
        mesh=mesh,
        in_specs=placed,
        out_specs=P("coil", None, "slab", None),
        check_vma=False,
    )
```

```python
import functools
import math

import jax
import jax.numpy as jnp
import numpy as np
from jax import lax
from jax.experimental import pallas as pl
from jax.experimental.pallas import tpu as pltpu
from jax.sharding import PartitionSpec as P

PHASES = 8
LANES = 128
UNROLL = 16
VLIM = 52
ROWS = 16
MESH = pl.DeviceIdType.MESH


def across(me, slab):
    half = slab // 2
    other = half - lax.div(me, half) * half
    return [other + i for i in range(half)]


def beside(me, slab):
    half = slab // 2
    first = lax.div(me, half) * half
    return [first + lax.rem(me + i, half) for i in range(1, half)]


def up(value, unit):
    return -(-value // unit) * unit


def dense_table(rows, row_ok, length):
    turns = rows[:, None].astype(np.int64) * np.arange(length)[None, :] % length
    angles = turns.astype(np.float64) * (2.0 * math.pi / length)
    scaling = row_ok[:, None] / math.sqrt(length)
    cos, sin = np.cos(angles) * scaling, np.sin(angles) * scaling
    return np.concatenate([cos, sin], 1), np.concatenate([-sin, cos], 1)


def kernel(
    dims,
    kspace_ref, maps_ref, index_ref, ky_ref, kz_ref, out_ref,
    raw, index, samples, grid, maps, ky_tab, kz_tab, send, recv, image, part_send, part_recv,
    in_sem, load_sem, send_sem, recv_sem, last_sem, own_sem, psend_sem, precv_sem,
):
    slab, coil, coils, offs, xr, kzb, kzp, lines, ny, yb, nz = dims
    me_s, me_c = lax.axis_index("slab"), lax.axis_index("coil")
    rows = 2 * coils * slab
    kzs = up(kzb, 8)
    chunks = xr // slab
    last = chunks - 1
    xo = xr // coil
    owners = slab // xo
    blocks = kzp // ROWS
    early = (blocks - 1) * ROWS
    woven = max(blocks - 2, 0)

    def chunk_of(k):
        own = lax.div(me_c, owners)
        if chunks % 2:
            return lax.rem(own + 1 + k, chunks)
        pair = lax.rem(lax.div(own, 2) + 1 + lax.div(k, 2), chunks // 2)
        return 2 * pair + lax.rem(own + 1 + k, 2)

    count = min(ROWS, kzb)

    def load_k(k, b):
        at = pl.ds(chunk_of(k) * slab, slab)
        planes = pl.ds(b * ROWS, count)
        return pltpu.make_async_copy(
            kspace_ref.at[:, :, :, at, planes], raw.at[:, :, :, at, planes], load_sem.at[k, b]
        )

    load_i = pltpu.make_async_copy(index_ref, index, in_sem.at[3])
    load_m = pltpu.make_async_copy(maps_ref, maps, in_sem.at[0])
    load_y = pltpu.make_async_copy(ky_ref, ky_tab, in_sem.at[1])
    load_z = pltpu.make_async_copy(kz_ref, kz_tab, in_sem.at[2])
    load_k(jnp.int32(0), 0).start()
    load_i.start()
    load_y.start()

    barrier = pltpu.get_barrier_semaphore()
    for o in range(1, slab):
        pl.semaphore_signal(
            barrier, inc=1, device_id={"slab": lax.rem(me_s + o, slab)}, device_id_type=MESH
        )
    for o in range(1, coil):
        pl.semaphore_signal(
            barrier, inc=1, device_id={"coil": lax.rem(me_c + o, coil)}, device_id_type=MESH
        )

    if kzp != kzb:
        grid[...] = jnp.zeros_like(grid)

    def unpack(first, b, i, carry):
        kz_at = pl.multiple_of(b * ROWS, ROWS)
        for c in range(coils):
            for t in range(offs):
                angle = 2.0 * math.pi * t / PHASES
                real = raw[0, c, t, first + i, pl.ds(kz_at, count)].astype(jnp.float32)
                imag = raw[1, c, t, first + i, pl.ds(kz_at, count)].astype(jnp.float32)
                if t:
                    cosine, sine = math.cos(angle), math.sin(angle)
                    real, imag = cosine * real + sine * imag, cosine * imag - sine * real
                for part, value in ((0, real), (1, imag)):
                    at = pl.multiple_of(((part * coils + c) * slab + i) * kzs + kz_at, 8)
                    samples[t, pl.ds(at, count), :] = value
        return carry

    ky_at = lax.broadcasted_iota(jnp.int32, (ny, offs * lines), 0)

    def place(first_kz, step, carry):
        kz = first_kz + step
        picked = jnp.concatenate([index[t, pl.ds(kz, 1), :] for t in range(offs)], axis=1)
        hot = jnp.where(ky_at == picked, 1.0, 0.0).astype(jnp.bfloat16)
        left = jnp.concatenate(
            [samples[t, pl.ds(kz, rows, stride=kzs), :].astype(jnp.bfloat16) for t in range(offs)],
            axis=1,
        )
        grid_at = pl.multiple_of(kz * rows, 8)
        placed = lax.dot_general(
            left, hot, (((1,), (1,)), ((), ())), preferred_element_type=jnp.float32
        )
        for j in range(ny // LANES):
            grid[j, pl.ds(grid_at, rows), :] = placed[:, j * LANES : (j + 1) * LANES]
        return carry


    def block_copy(k, b, c, d, arrived):
        planes = pl.ds(pl.multiple_of(b * ROWS, ROWS), ROWS)
        return pltpu.make_async_remote_copy(
            src_ref=send.at[k, c, d, :, planes],
            dst_ref=recv.at[k, c, me_s, :, planes],
            send_sem=send_sem.at[k],
            recv_sem=arrived,
            device_id={"slab": d},
            device_id_type=MESH,
        )

    def all_of(k, c, planes, arrived):
        return pltpu.make_async_remote_copy(
            src_ref=recv.at[k, c, pl.ds(0, slab - 1), :, planes],
            dst_ref=recv.at[k, c, pl.ds(0, slab - 1), :, planes],
            send_sem=send_sem.at[k],
            recv_sem=arrived,
            device_id={"slab": lax.rem(me_s + 1, slab)},
            device_id_type=MESH,
        )

    def all_sent(k):
        return pltpu.make_async_remote_copy(
            src_ref=send.at[k, :, pl.ds(0, slab - 1)],
            dst_ref=recv.at[k, :, pl.ds(0, slab - 1)],
            send_sem=send_sem.at[k],
            recv_sem=recv_sem.at[k, 0],
            device_id={"slab": lax.rem(me_s + 1, slab)},
            device_id_type=MESH,
        )

    def own_copy(k, c):
        return pltpu.make_async_copy(send.at[k, c, me_s], recv.at[k, c, me_s], own_sem.at[k, c])

    lane = lax.broadcasted_iota(jnp.int32, (ROWS, LANES), 1)

    def rows_pass(k, b, c, carry):
        kz_at = pl.multiple_of(b * ROWS, ROWS)
        lefts = []
        for i in range(slab):
            pieces = []
            for part in range(2):
                at = (part * coils + c) * slab + i
                for j in range(ny // LANES):
                    here = grid[j, pl.ds(kz_at * rows + at, ROWS, stride=rows), :]
                    pieces.append(here.astype(jnp.bfloat16))
            lefts.append(jnp.concatenate(pieces, axis=1))
        hybrid = jnp.dot(
            jnp.concatenate(lefts, axis=0), ky_tab[...], preferred_element_type=jnp.float32
        )
        for part in range(2):
            turned = []
            for i in range(slab):
                value = hybrid[i * ROWS : (i + 1) * ROWS, part * ny : (part + 1) * ny]
                turned.append(pltpu.roll(value, i * yb, 1) if i else value)
            for d in range(slab):
                for j in range(ny // LANES):
                    low, high = j * LANES // yb, ((j + 1) * LANES - 1) // yb
                    cut = slice(j * LANES, (j + 1) * LANES)
                    tile = turned[(low - d) % slab][:, cut]
                    for p in range(low + 1, high + 1):
                        tile = jnp.where(
                            lane >= p * yb - j * LANES, turned[(p - d) % slab][:, cut], tile
                        )
                    send[k, c, d, part, pl.ds(kz_at, ROWS), cut] = tile.astype(jnp.bfloat16)

        @pl.when((k == 0) & (b == 0) & (c == 0))
        def _():
            pl.semaphore_wait(barrier, slab + coil - 2)

        @pl.when((k < last) | (b < woven))
        def _():
            for d in across(me_s, slab) + beside(me_s, slab):
                block_copy(k, b, c, d, recv_sem.at[k, c]).start()

        @pl.when(b == blocks - 1)
        def _():
            own_copy(k, c).start()

        return carry

    def chunk_pass(k, carry):
        first = chunk_of(k) * slab

        def block_pass(b, inner):
            load_k(k, b).wait()
            lax.fori_loop(0, slab, functools.partial(unpack, first, b), 0)
            lax.fori_loop(0, count, functools.partial(place, b * ROWS), 0, unroll=UNROLL)

            @pl.when((k == 0) & (b == 0))
            def _():
                load_y.wait()

            lax.fori_loop(0, coils, functools.partial(rows_pass, k, b), 0)

            @pl.when((k == 0) & (b == 0))
            def _():
                for j in range(1, chunks * blocks):
                    load_k(jnp.int32(j // blocks), j % blocks).start()
                load_m.start()
                load_z.start()

            return inner

        return lax.fori_loop(0, blocks, block_pass, carry)

    load_i.wait()
    lax.fori_loop(0, chunks, chunk_pass, 0)
    far, near = across(me_s, slab), beside(me_s, slab)
    middle = len(far) // 2
    ends = range(woven, blocks)
    order = [(d, b) for d in far[:middle] + near for b in ends]
    order += [(d, b) for b in ends for d in far[middle:]]
    for d, b in order:
        for c in range(coils):
            arrived = recv_sem.at[last, c] if b < blocks - 1 else last_sem.at[c]
            block_copy(last, b, c, d, arrived).start()
    load_m.wait()
    load_z.wait()

    def part_copy(k, q):
        owner = chunk_of(k) * owners + q
        return pltpu.make_async_remote_copy(
            src_ref=part_send.at[chunk_of(k), pl.ds(q * xo, xo)],
            dst_ref=part_recv.at[lax.rem(owner - me_c + coil, coil)],
            send_sem=psend_sem.at[k, q],
            recv_sem=precv_sem.at[lax.rem(owner - me_c + coil, coil)],
            device_id={"coil": owner},
            device_id_type=MESH,
        )

    def depth(k, c, at, planes):
        block = recv[k, c, :, :, pl.ds(at, planes)].reshape(slab * 2 * planes, slab * yb)
        table = kz_tab[:, :, pl.ds(at, planes)].reshape(slab * 2 * planes, 2 * nz)
        return lax.dot_general(
            block, table, (((0,), (0,)), ((), ())), preferred_element_type=jnp.float32
        )

    def combined(c, p, x):
        real = image[c, pl.ds(p * yb, yb), :nz]
        imag = image[c, pl.ds(p * yb, yb), nz:]
        map_real = maps[0, c, x].astype(jnp.float32)
        map_imag = maps[1, c, x].astype(jnp.float32)
        return map_real * real + map_imag * imag, map_real * imag - map_imag * real

    def depth_pass(k, carry):
        first = chunk_of(k) * slab

        def one_coil(c, inner):
            own_copy(k, c).wait()
            @pl.when(k < last)
            def _():
                all_of(k, c, pl.ds(0, kzp), recv_sem.at[k, c]).wait_recv()

            image[c] = depth(k, c, 0, kzp)
            return inner

        lax.fori_loop(0, coils, one_coil, 0)
        for p in range(slab):
            x = lax.rem(p - me_s + slab, slab)
            add_real, add_imag = combined(0, p, first + x)
            for c in range(1, coils):
                term_real, term_imag = combined(c, p, first + x)
                add_real, add_imag = add_real + term_real, add_imag + term_imag
            part_send[chunk_of(k), x, 0] = add_real.astype(jnp.bfloat16)
            part_send[chunk_of(k), x, 1] = add_imag.astype(jnp.bfloat16)
        for q in range(owners):
            @pl.when(chunk_of(k) * owners + q != me_c)
            def _():
                part_copy(k, q).start()
        return carry

    def wait_parts():
        for o in range(1, coil):
            pltpu.make_async_remote_copy(
                src_ref=part_recv.at[o],
                dst_ref=part_recv.at[o],
                send_sem=psend_sem.at[0, 0],
                recv_sem=precv_sem.at[o],
                device_id={"coil": lax.rem(me_c + o, coil)},
                device_id_type=MESH,
            ).wait_recv()

    def drain(k, carry):
        all_sent(k).wait_send()
        for q in range(owners):
            @pl.when(chunk_of(k) * owners + q != me_c)
            def _():
                part_copy(k, q).wait_send()
        return carry

    own_chunk = lax.div(me_c, owners)

    if owners == 1 and coil > 1:
        lax.fori_loop(0, last, depth_pass, 0)
        wait_parts()

        def add_up(c):
            for p in range(slab):
                x = lax.rem(p - me_s + slab, slab)
                add_real, add_imag = combined(c, p, own_chunk * slab + x)
                out_ref[x, 0] += add_real
                out_ref[x, 1] += add_imag

        def total(i, carry):
            value = part_recv[1, i].astype(jnp.float32)
            for o in range(2, coil):
                value = value + part_recv[o, i].astype(jnp.float32)
            out_ref[i] = value
            return carry

        lax.fori_loop(0, xo, total, 0)
        for c in range(coils):
            own_copy(last, c).wait()
        if blocks > 1:
            for c in range(coils):
                all_of(last, c, pl.ds(0, early), recv_sem.at[last, c]).wait_recv()
                image[c] = depth(last, c, 0, early)
            for c in range(coils):
                add_up(c)
        lax.fori_loop(0, last, drain, 0)
        for c in range(coils):
            all_of(last, c, pl.ds(early, ROWS), last_sem.at[c]).wait_recv()
            image[c] = depth(last, c, early, ROWS)
            add_up(c)
        drain(last, 0)
    else:

        lax.fori_loop(0, last, depth_pass, 0)
        for c in range(coils):
            if blocks > 1:
                all_of(last, c, pl.ds(0, early), recv_sem.at[last, c]).wait_recv()
            all_of(last, c, pl.ds(early, ROWS), last_sem.at[c]).wait_recv()
        depth_pass(last, 0)
        wait_parts()
        own_at = lax.rem(me_c, owners) * xo

        def total(i, carry):
            value = part_send[own_chunk, own_at + i].astype(jnp.float32)
            for o in range(1, coil):
                value = value + part_recv[o, i].astype(jnp.float32)
            out_ref[i] = value
            return carry

        lax.fori_loop(0, xo, total, 0)
        lax.fori_loop(0, chunks, drain, 0)


def local(mesh, kspace, coil_maps, line_index):
    slab, coil = mesh.shape["slab"], mesh.shape["coil"]
    _, coils, offs, xr, kzb, lines = kspace.shape
    yb, nz = coil_maps.shape[3:]
    ny = yb * slab
    kzp = up(kzb, 16)
    dims = (slab, coil, coils, offs, xr, kzb, kzp, lines, ny, yb, nz)
    chunks, xo = xr // slab, xr // coil
    owners = slab // xo
    rows = 2 * coils * slab
    f32, bf16 = jnp.float32, jnp.bfloat16

    ky_table = np.concatenate(dense_table(np.arange(ny), np.ones(ny), ny), 0)
    local_kz = np.arange(kzp)
    per_slab = []
    for s in range(slab):
        per_slab += dense_table(s * kzb + local_kz, (local_kz < kzb) * 1.0, nz)
    kz_table = np.concatenate(per_slab, 0).reshape(slab, 2, kzp, 2 * nz)
    ky_table = jnp.asarray(ky_table.astype(np.float32)).astype(bf16)
    kz_table = jnp.asarray(kz_table.astype(np.float32)).astype(bf16)

    vmem, hbm = pl.BlockSpec(memory_space=pltpu.VMEM), pl.BlockSpec(memory_space=pltpu.HBM)
    dma = pltpu.SemaphoreType.DMA
    return pl.pallas_call(
        functools.partial(kernel, dims),
        out_shape=jax.ShapeDtypeStruct((xo, 2, yb, nz), f32),
        in_specs=[hbm] * 5,
        out_specs=vmem,
        scratch_shapes=[
            pltpu.VMEM(kspace.shape, bf16),
            pltpu.VMEM(line_index.shape, jnp.int32),
            pltpu.VMEM((offs, rows * up(kzb, 8), lines), f32),
            pltpu.VMEM((ny // LANES, kzp * rows, LANES), f32),
            pltpu.VMEM(coil_maps.shape, bf16),
            pltpu.VMEM(ky_table.shape, bf16),
            pltpu.VMEM(kz_table.shape, bf16),
            pltpu.VMEM((chunks, coils, slab, 2, kzp, ny), bf16),
            pltpu.VMEM((chunks, coils, slab, 2, kzp, ny), bf16),
            pltpu.VMEM((coils, ny, 2 * nz), f32),
            pltpu.VMEM((chunks, slab, 2, yb, nz), bf16),
            pltpu.VMEM((coil, xo, 2, yb, nz), bf16),
            dma((4,)),
            dma((chunks, kzp // ROWS)),
            dma((chunks,)),
            dma((chunks, coils)),
            dma((coils,)),
            dma((chunks, coils)),
            dma((chunks, owners)),
            dma((coil,)),
        ],
        compiler_params=pltpu.CompilerParams(
            collective_id=0, has_side_effects=True, vmem_limit_bytes=VLIM * 1024 * 1024
        ),
    )(kspace, coil_maps, pltpu.with_memory_space_constraint(line_index, pltpu.HBM), ky_table, kz_table)


def solution(mesh):
    placed = (
        P(None, "coil", None, None, "slab", None),
        P(None, "coil", None, "slab", None),
        P(None, "slab", None),
    )
    return jax.shard_map(
        functools.partial(local, mesh),
        mesh=mesh,
        in_specs=placed,
        out_specs=P("coil", None, "slab", None),
        check_vma=False,
    )
```

```python
import functools
import math

import jax
import jax.numpy as jnp
import numpy as np
from jax import lax
from jax.experimental import pallas as pl
from jax.experimental.pallas import tpu as pltpu
from jax.sharding import PartitionSpec as P

PHASES = 8
LANES = 128
UNROLL = 16
VLIM = 52
ROWS = 16
HALF = 8
MESH = pl.DeviceIdType.MESH


def across(me, slab):
    half = slab // 2
    other = half - lax.div(me, half) * half
    return [other + i for i in range(half)]


def beside(me, slab):
    half = slab // 2
    first = lax.div(me, half) * half
    return [first + lax.rem(me + i, half) for i in range(1, half)]


def up(value, unit):
    return -(-value // unit) * unit


def dense_table(rows, row_ok, length):
    turns = rows[:, None].astype(np.int64) * np.arange(length)[None, :] % length
    angles = turns.astype(np.float64) * (2.0 * math.pi / length)
    scaling = row_ok[:, None] / math.sqrt(length)
    cos, sin = np.cos(angles) * scaling, np.sin(angles) * scaling
    return np.concatenate([cos, sin], 1), np.concatenate([-sin, cos], 1)


def kernel(
    dims,
    kspace_ref, maps_ref, index_ref, ky_ref, kz_ref, out_ref,
    raw, index, samples, grid, maps, ky_tab, kz_tab, send, recv, image, part_send, part_recv,
    in_sem, load_sem, send_sem, recv_sem, last_sem, own_sem, psend_sem, precv_sem,
):
    slab, coil, coils, offs, xr, kzb, kzp, lines, ny, yb, nz = dims
    me_s, me_c = lax.axis_index("slab"), lax.axis_index("coil")
    rows = 2 * coils * slab
    kzs = up(kzb, 8)
    chunks = xr // slab
    last = chunks - 1
    xo = xr // coil
    owners = slab // xo
    blocks = kzp // ROWS
    early = (blocks - 1) * ROWS
    woven = max(blocks - 2, 0)
    split = last > 0 and kzb % ROWS == 0

    barrier = pltpu.get_barrier_semaphore()
    for d in across(me_s, slab) + beside(me_s, slab):
        pl.semaphore_signal(barrier, inc=1, device_id={"slab": d}, device_id_type=MESH)
    for o in range(1, coil):
        pl.semaphore_signal(
            barrier, inc=1, device_id={"coil": lax.rem(me_c + o, coil)}, device_id_type=MESH
        )

    def chunk_of(k):
        own = lax.div(me_c, owners)
        if chunks % 2:
            return lax.rem(own + 1 + k, chunks)
        pair = lax.rem(lax.div(own, 2) + 1 + lax.div(k, 2), chunks // 2)
        return 2 * pair + lax.rem(own + 1 + k, 2)

    count = min(ROWS, kzb)

    def load_k(k, b):
        at = pl.ds(chunk_of(k) * slab, slab)
        planes = pl.ds(b * ROWS, count)
        return pltpu.make_async_copy(
            kspace_ref.at[:, :, :, at, planes], raw.at[:, :, :, at, planes], load_sem.at[k, b]
        )

    load_i = pltpu.make_async_copy(index_ref, index, in_sem.at[3])
    load_m = pltpu.make_async_copy(maps_ref, maps, in_sem.at[0])
    load_y = pltpu.make_async_copy(ky_ref, ky_tab, in_sem.at[1])
    load_z = pltpu.make_async_copy(kz_ref, kz_tab, in_sem.at[2])
    load_k(jnp.int32(0), 0).start()
    load_i.start()
    load_y.start()
    for b in range(1, blocks):
        load_k(jnp.int32(0), b).start()

    if kzp != kzb:
        grid[...] = jnp.zeros_like(grid)

    def unpack(first, b, i, carry):
        kz_at = pl.multiple_of(b * ROWS, ROWS)
        for c in range(coils):
            for t in range(offs):
                angle = 2.0 * math.pi * t / PHASES
                real = raw[0, c, t, first + i, pl.ds(kz_at, count)].astype(jnp.float32)
                imag = raw[1, c, t, first + i, pl.ds(kz_at, count)].astype(jnp.float32)
                if t:
                    cosine, sine = math.cos(angle), math.sin(angle)
                    real, imag = cosine * real + sine * imag, cosine * imag - sine * real
                for part, value in ((0, real), (1, imag)):
                    at = pl.multiple_of(((part * coils + c) * slab + i) * kzs + kz_at, 8)
                    samples[t, pl.ds(at, count), :] = value
        return carry

    ky_at = lax.broadcasted_iota(jnp.int32, (ny, offs * lines), 0)

    def place(first_kz, step, carry):
        kz = first_kz + step
        picked = jnp.concatenate([index[t, pl.ds(kz, 1), :] for t in range(offs)], axis=1)
        hot = jnp.where(ky_at == picked, 1.0, 0.0).astype(jnp.bfloat16)
        left = jnp.concatenate(
            [samples[t, pl.ds(kz, rows, stride=kzs), :].astype(jnp.bfloat16) for t in range(offs)],
            axis=1,
        )
        grid_at = pl.multiple_of(kz * rows, 8)
        placed = lax.dot_general(
            left, hot, (((1,), (1,)), ((), ())), preferred_element_type=jnp.float32
        )
        for j in range(ny // LANES):
            grid[j, pl.ds(grid_at, rows), :] = placed[:, j * LANES : (j + 1) * LANES]
        return carry


    def tiles(first, planes):
        return pl.ds(lax.div(first, HALF), planes // HALF)

    def block_copy(k, first, planes, c, d, arrived):
        return pltpu.make_async_remote_copy(
            src_ref=send.at[k, c, d, tiles(first, planes)],
            dst_ref=recv.at[k, c, me_s, tiles(first, planes)],
            send_sem=send_sem.at[k],
            recv_sem=arrived,
            device_id={"slab": d},
            device_id_type=MESH,
        )

    def all_of(k, c, planes, arrived):
        return pltpu.make_async_remote_copy(
            src_ref=recv.at[k, c, pl.ds(0, slab - 1), planes],
            dst_ref=recv.at[k, c, pl.ds(0, slab - 1), planes],
            send_sem=send_sem.at[k],
            recv_sem=arrived,
            device_id={"slab": lax.rem(me_s + 1, slab)},
            device_id_type=MESH,
        )

    def all_sent(k):
        return pltpu.make_async_remote_copy(
            src_ref=send.at[k, :, pl.ds(0, slab - 1)],
            dst_ref=recv.at[k, :, pl.ds(0, slab - 1)],
            send_sem=send_sem.at[k],
            recv_sem=recv_sem.at[k, 0],
            device_id={"slab": lax.rem(me_s + 1, slab)},
            device_id_type=MESH,
        )

    def own_copy(k, c):
        return pltpu.make_async_copy(send.at[k, c, me_s], recv.at[k, c, me_s], own_sem.at[k, c])

    lane = lax.broadcasted_iota(jnp.int32, (ROWS, LANES), 1)

    def rows_pass(k, c, first, planes):
        lefts = []
        for i in range(slab):
            pieces = []
            for part in range(2):
                at = (part * coils + c) * slab + i
                for j in range(ny // LANES):
                    pieces.append(grid[j, pl.ds(first * rows + at, planes, stride=rows), :])
            lefts.append(jnp.concatenate(pieces, axis=1))
        hybrid = jnp.dot(
            jnp.concatenate(lefts, axis=0).astype(jnp.bfloat16),
            ky_tab[...],
            preferred_element_type=jnp.float32,
        )
        turned = []
        for part in range(2):
            values = []
            for i in range(slab):
                value = hybrid[i * planes : (i + 1) * planes, part * ny : (part + 1) * ny]
                values.append(pltpu.roll(value, i * yb, 1) if i else value)
            turned.append(values)
        for d in range(slab):
            for j in range(ny // LANES):
                low, high = j * LANES // yb, ((j + 1) * LANES - 1) // yb
                cut = slice(j * LANES, (j + 1) * LANES)
                parts = []
                for values in turned:
                    tile = values[(low - d) % slab][:, cut]
                    for p in range(low + 1, high + 1):
                        tile = jnp.where(
                            lane[:planes] >= p * yb - j * LANES, values[(p - d) % slab][:, cut], tile
                        )
                    parts.append(tile)
                for g in range(planes // HALF):
                    both = [tile[g * HALF : (g + 1) * HALF] for tile in parts]
                    send[k, c, d, lax.div(first, HALF) + g, :, cut] = jnp.concatenate(
                        both, axis=0
                    ).astype(jnp.bfloat16)

    def send_rows(k, c, first, planes):
        for d in across(me_s, slab) + beside(me_s, slab):
            block_copy(k, first, planes, c, d, recv_sem.at[k, c]).start()

    def fill(k, b):
        load_k(k, b).wait()
        lax.fori_loop(0, slab, functools.partial(unpack, chunk_of(k) * slab, b), 0)

    def later_loads():
        for j in range(blocks, chunks * blocks):
            load_k(jnp.int32(j // blocks), j % blocks).start()
        load_m.start()
        load_z.start()

    def block_pass(j, carry):
        k, b = lax.div(j, blocks), lax.rem(j, blocks)
        first = pl.multiple_of(b * ROWS, ROWS)
        fill(k, b)
        lax.fori_loop(0, count, functools.partial(place, first), 0, unroll=UNROLL)
        if not split:

            @pl.when(j == 0)
            def _():
                load_y.wait()

        def one_coil(c, inner):
            rows_pass(k, c, first, ROWS)

            @pl.when(((k == 0) & (last > 0)) | ((k == last) & (b < woven)))
            def _():
                send_rows(k, c, first, ROWS)

            @pl.when(b == blocks - 1)
            def _():
                own_copy(k, c).start()

            return inner

        if not split:

            @pl.when(j == 0)
            def _():
                pl.semaphore_wait(barrier, slab + coil - 2)
                later_loads()

        lax.fori_loop(0, coils, one_coil, 0)

        @pl.when((k > 0) & (k < last) & (b == blocks - 1))
        def _():
            for d in across(me_s, slab) + beside(me_s, slab):
                for c in range(coils):
                    block_copy(k, 0, kzp, c, d, recv_sem.at[k, c]).start()

        return carry

    def half_pass(q, carry):
        first = pl.multiple_of(lax.div(q, coils) * HALF, HALF)
        c = lax.rem(q, coils)

        @pl.when(c == 0)
        def _():
            lax.fori_loop(0, HALF, functools.partial(place, first), 0, unroll=HALF)

        @pl.when(q == 0)
        def _():
            load_y.wait()

        rows_pass(0, c, first, HALF)

        @pl.when(q == 0)
        def _():
            pl.semaphore_wait(barrier, slab + coil - 2)

        send_rows(0, c, first, HALF)
        return carry

    load_i.wait()
    if split:
        fill(jnp.int32(0), 0)
        lax.fori_loop(0, coils * (ROWS // HALF), half_pass, 0)
        later_loads()
        if blocks == 1:
            for c in range(coils):
                own_copy(0, c).start()
    lax.fori_loop(int(split), chunks * blocks, block_pass, 0)
    far, near = across(me_s, slab), beside(me_s, slab)
    middle = len(far) // 2
    ends = range(woven, blocks)
    order = [(d, b) for d in far[:middle] + near for b in ends]
    order += [(d, b) for b in ends for d in far[middle:]]
    for d, b in order:
        for c in range(coils):
            arrived = recv_sem.at[last, c] if b < blocks - 1 else last_sem.at[c]
            block_copy(last, b * ROWS, ROWS, c, d, arrived).start()
    load_m.wait()
    load_z.wait()

    def part_copy(k, q):
        owner = chunk_of(k) * owners + q
        return pltpu.make_async_remote_copy(
            src_ref=part_send.at[chunk_of(k), pl.ds(q * xo, xo)],
            dst_ref=part_recv.at[lax.rem(owner - me_c + coil, coil)],
            send_sem=psend_sem.at[k, q],
            recv_sem=precv_sem.at[lax.rem(owner - me_c + coil, coil)],
            device_id={"coil": owner},
            device_id_type=MESH,
        )

    def depth(k, c, at, planes):
        block = recv[k, c, :, tiles(at, planes)].reshape(slab * 2 * planes, slab * yb)
        table = kz_tab[:, tiles(at, planes)].reshape(slab * 2 * planes, 2 * nz)
        return lax.dot_general(
            block, table, (((0,), (0,)), ((), ())), preferred_element_type=jnp.float32
        )

    def combined(c, p, x):
        real = image[c, pl.ds(p * yb, yb), :nz]
        imag = image[c, pl.ds(p * yb, yb), nz:]
        map_real = maps[0, c, x].astype(jnp.float32)
        map_imag = maps[1, c, x].astype(jnp.float32)
        return map_real * real + map_imag * imag, map_real * imag - map_imag * real

    def depth_pass(k, carry):
        first = chunk_of(k) * slab

        def one_coil(c, inner):
            own_copy(k, c).wait()
            @pl.when(k < last)
            def _():
                all_of(k, c, tiles(0, kzp), recv_sem.at[k, c]).wait_recv()

            image[c] = depth(k, c, 0, kzp)
            return inner

        lax.fori_loop(0, coils, one_coil, 0)
        for p in range(slab):
            x = lax.rem(p - me_s + slab, slab)
            add_real, add_imag = combined(0, p, first + x)
            for c in range(1, coils):
                term_real, term_imag = combined(c, p, first + x)
                add_real, add_imag = add_real + term_real, add_imag + term_imag
            part_send[chunk_of(k), x, 0] = add_real.astype(jnp.bfloat16)
            part_send[chunk_of(k), x, 1] = add_imag.astype(jnp.bfloat16)
        for q in range(owners):
            @pl.when(chunk_of(k) * owners + q != me_c)
            def _():
                part_copy(k, q).start()
        return carry

    def wait_parts():
        for o in range(1, coil):
            pltpu.make_async_remote_copy(
                src_ref=part_recv.at[o],
                dst_ref=part_recv.at[o],
                send_sem=psend_sem.at[0, 0],
                recv_sem=precv_sem.at[o],
                device_id={"coil": lax.rem(me_c + o, coil)},
                device_id_type=MESH,
            ).wait_recv()

    def drain(k, carry):
        all_sent(k).wait_send()
        for q in range(owners):
            @pl.when(chunk_of(k) * owners + q != me_c)
            def _():
                part_copy(k, q).wait_send()
        return carry

    own_chunk = lax.div(me_c, owners)

    if owners == 1 and coil > 1:
        lax.fori_loop(0, last, depth_pass, 0)
        wait_parts()

        def add_up(c):
            for p in range(slab):
                x = lax.rem(p - me_s + slab, slab)
                add_real, add_imag = combined(c, p, own_chunk * slab + x)
                out_ref[x, 0] += add_real
                out_ref[x, 1] += add_imag

        def total(i, carry):
            value = part_recv[1, i].astype(jnp.float32)
            for o in range(2, coil):
                value = value + part_recv[o, i].astype(jnp.float32)
            out_ref[i] = value
            return carry

        lax.fori_loop(0, xo, total, 0)
        for c in range(coils):
            own_copy(last, c).wait()
        if blocks > 1:
            for c in range(coils):
                all_of(last, c, tiles(0, early), recv_sem.at[last, c]).wait_recv()
                image[c] = depth(last, c, 0, early)
            for c in range(coils):
                add_up(c)
        lax.fori_loop(0, last, drain, 0)
        for c in range(coils):
            all_of(last, c, tiles(early, ROWS), last_sem.at[c]).wait_recv()
            image[c] = depth(last, c, early, ROWS)
            add_up(c)
        drain(last, 0)
    else:

        lax.fori_loop(0, last, depth_pass, 0)
        for c in range(coils):
            if blocks > 1:
                all_of(last, c, tiles(0, early), recv_sem.at[last, c]).wait_recv()
            all_of(last, c, tiles(early, ROWS), last_sem.at[c]).wait_recv()
        depth_pass(last, 0)
        wait_parts()
        own_at = lax.rem(me_c, owners) * xo

        def total(i, carry):
            value = part_send[own_chunk, own_at + i].astype(jnp.float32)
            for o in range(1, coil):
                value = value + part_recv[o, i].astype(jnp.float32)
            out_ref[i] = value
            return carry

        lax.fori_loop(0, xo, total, 0)
        lax.fori_loop(0, chunks, drain, 0)


def local(mesh, kspace, coil_maps, line_index):
    slab, coil = mesh.shape["slab"], mesh.shape["coil"]
    _, coils, offs, xr, kzb, lines = kspace.shape
    yb, nz = coil_maps.shape[3:]
    ny = yb * slab
    kzp = up(kzb, 16)
    dims = (slab, coil, coils, offs, xr, kzb, kzp, lines, ny, yb, nz)
    chunks, xo = xr // slab, xr // coil
    owners = slab // xo
    rows = 2 * coils * slab
    f32, bf16 = jnp.float32, jnp.bfloat16

    ky_table = np.concatenate(dense_table(np.arange(ny), np.ones(ny), ny), 0)
    local_kz = np.arange(kzp)
    per_slab = []
    for s in range(slab):
        per_slab += dense_table(s * kzb + local_kz, (local_kz < kzb) * 1.0, nz)
    kz_table = np.concatenate(per_slab, 0).reshape(slab, 2, kzp // HALF, HALF, 2 * nz)
    kz_table = kz_table.swapaxes(1, 2).reshape(slab, kzp // HALF, 2 * HALF, 2 * nz)
    ky_table = jnp.asarray(ky_table.astype(np.float32)).astype(bf16)
    kz_table = jnp.asarray(kz_table.astype(np.float32)).astype(bf16)

    vmem, hbm = pl.BlockSpec(memory_space=pltpu.VMEM), pl.BlockSpec(memory_space=pltpu.HBM)
    dma = pltpu.SemaphoreType.DMA
    return pl.pallas_call(
        functools.partial(kernel, dims),
        out_shape=jax.ShapeDtypeStruct((xo, 2, yb, nz), f32),
        in_specs=[hbm] * 5,
        out_specs=vmem,
        scratch_shapes=[
            pltpu.VMEM(kspace.shape, bf16),
            pltpu.VMEM(line_index.shape, jnp.int32),
            pltpu.VMEM((offs, rows * up(kzb, 8), lines), f32),
            pltpu.VMEM((ny // LANES, kzp * rows, LANES), f32),
            pltpu.VMEM(coil_maps.shape, bf16),
            pltpu.VMEM(ky_table.shape, bf16),
            pltpu.VMEM(kz_table.shape, bf16),
            pltpu.VMEM((chunks, coils, slab, kzp // HALF, 2 * HALF, ny), bf16),
            pltpu.VMEM((chunks, coils, slab, kzp // HALF, 2 * HALF, ny), bf16),
            pltpu.VMEM((coils, ny, 2 * nz), f32),
            pltpu.VMEM((chunks, slab, 2, yb, nz), bf16),
            pltpu.VMEM((coil, xo, 2, yb, nz), bf16),
            dma((4,)),
            dma((chunks, kzp // ROWS)),
            dma((chunks,)),
            dma((chunks, coils)),
            dma((coils,)),
            dma((chunks, coils)),
            dma((chunks, owners)),
            dma((coil,)),
        ],
        compiler_params=pltpu.CompilerParams(
            collective_id=0, has_side_effects=True, vmem_limit_bytes=VLIM * 1024 * 1024
        ),
    )(kspace, coil_maps, pltpu.with_memory_space_constraint(line_index, pltpu.HBM), ky_table, kz_table)


def solution(mesh):
    placed = (
        P(None, "coil", None, None, "slab", None),
        P(None, "coil", None, "slab", None),
        P(None, "slab", None),
    )
    return jax.shard_map(
        functools.partial(local, mesh),
        mesh=mesh,
        in_specs=placed,
        out_specs=P("coil", None, "slab", None),
        check_vma=False,
    )
```

```python
import functools
import math

import jax
import jax.numpy as jnp
import numpy as np
from jax import lax
from jax.experimental import pallas as pl
from jax.experimental.pallas import tpu as pltpu
from jax.sharding import PartitionSpec as P

PHASES = 8
LANES = 128
UNROLL = 16
VLIM = 48
FINISH = 8
ROWS = 16
HALF = 8
MESH = pl.DeviceIdType.MESH


def across(me, slab):
    half = slab // 2
    other = half - lax.div(me, half) * half
    return [other + i for i in range(half)]


def beside(me, slab):
    half = slab // 2
    first = lax.div(me, half) * half
    return [first + lax.rem(me + i, half) for i in range(1, half)]


def up(value, unit):
    return -(-value // unit) * unit


def dense_table(rows, row_ok, length):
    turns = rows[:, None].astype(np.int64) * np.arange(length)[None, :] % length
    angles = turns.astype(np.float64) * (2.0 * math.pi / length)
    scaling = row_ok[:, None] / math.sqrt(length)
    cos, sin = np.cos(angles) * scaling, np.sin(angles) * scaling
    return np.concatenate([cos, sin], 1), np.concatenate([-sin, cos], 1)


def kernel(
    dims,
    kspace_ref, maps_ref, index_ref, ky_ref, kz_ref, out_ref, block_ref, held_maps, held_table,
    raw, index, samples, grid, maps, ky_tab, kz_tab, send, recv, image, part_send, part_recv,
    in_sem, load_sem, send_sem, recv_sem, last_sem, own_sem, psend_sem, precv_sem,
):
    slab, coil, coils, offs, xr, kzb, kzp, lines, ny, yb, nz = dims
    me_s, me_c = lax.axis_index("slab"), lax.axis_index("coil")
    rows = 2 * coils * slab
    kzs = up(kzb, 8)
    chunks = xr // slab
    last = chunks - 1
    xo = xr // coil
    owners = slab // xo
    blocks = kzp // ROWS
    early = (blocks - 1) * ROWS
    woven = max(blocks - 2, 0)
    split = last > 0 and kzb % ROWS == 0

    barrier = pltpu.get_barrier_semaphore()
    for d in across(me_s, slab) + beside(me_s, slab):
        pl.semaphore_signal(barrier, inc=1, device_id={"slab": d}, device_id_type=MESH)
    for o in range(1, coil):
        pl.semaphore_signal(
            barrier, inc=1, device_id={"coil": lax.rem(me_c + o, coil)}, device_id_type=MESH
        )

    def chunk_of(k):
        own = lax.div(me_c, owners)
        if chunks % 2:
            return lax.rem(own + 1 + k, chunks)
        pair = lax.rem(lax.div(own, 2) + 1 + lax.div(k, 2), chunks // 2)
        return 2 * pair + lax.rem(own + 1 + k, 2)

    count = min(ROWS, kzb)

    def load_k(k, b):
        at = pl.ds(chunk_of(k) * slab, slab)
        planes = pl.ds(b * ROWS, count)
        return pltpu.make_async_copy(
            kspace_ref.at[:, :, :, at, planes], raw.at[:, :, :, at, planes], load_sem.at[k, b]
        )

    load_i = pltpu.make_async_copy(index_ref, index, in_sem.at[3])
    load_m = pltpu.make_async_copy(maps_ref, maps, in_sem.at[0])
    load_y = pltpu.make_async_copy(ky_ref, ky_tab, in_sem.at[1])
    load_z = pltpu.make_async_copy(kz_ref, kz_tab, in_sem.at[2])
    load_k(jnp.int32(0), 0).start()
    load_i.start()
    load_y.start()
    for b in range(1, blocks):
        load_k(jnp.int32(0), b).start()

    if kzp != kzb:
        grid[...] = jnp.zeros_like(grid)

    def unpack(first, b, i, carry):
        kz_at = pl.multiple_of(b * ROWS, ROWS)
        for c in range(coils):
            for t in range(offs):
                angle = 2.0 * math.pi * t / PHASES
                real = raw[0, c, t, first + i, pl.ds(kz_at, count)].astype(jnp.float32)
                imag = raw[1, c, t, first + i, pl.ds(kz_at, count)].astype(jnp.float32)
                if t:
                    cosine, sine = math.cos(angle), math.sin(angle)
                    real, imag = cosine * real + sine * imag, cosine * imag - sine * real
                for part, value in ((0, real), (1, imag)):
                    at = pl.multiple_of(((part * coils + c) * slab + i) * kzs + kz_at, 8)
                    samples[t, pl.ds(at, count), :] = value
        return carry

    ky_at = lax.broadcasted_iota(jnp.int32, (ny, offs * lines), 0)

    def place(first_kz, step, carry):
        kz = first_kz + step
        picked = jnp.concatenate([index[t, pl.ds(kz, 1), :] for t in range(offs)], axis=1)
        hot = jnp.where(ky_at == picked, 1.0, 0.0).astype(jnp.bfloat16)
        left = jnp.concatenate(
            [samples[t, pl.ds(kz, rows, stride=kzs), :].astype(jnp.bfloat16) for t in range(offs)],
            axis=1,
        )
        grid_at = pl.multiple_of(kz * rows, 8)
        placed = lax.dot_general(
            left, hot, (((1,), (1,)), ((), ())), preferred_element_type=jnp.float32
        )
        for j in range(ny // LANES):
            grid[j, pl.ds(grid_at, rows), :] = placed[:, j * LANES : (j + 1) * LANES]
        return carry


    def tiles(first, planes):
        return pl.ds(lax.div(first, HALF), planes // HALF)

    def block_copy(k, first, planes, c, d, arrived):
        return pltpu.make_async_remote_copy(
            src_ref=send.at[k, c, d, tiles(first, planes)],
            dst_ref=recv.at[k, c, me_s, tiles(first, planes)],
            send_sem=send_sem.at[k],
            recv_sem=arrived,
            device_id={"slab": d},
            device_id_type=MESH,
        )

    def all_of(k, c, planes, arrived):
        return pltpu.make_async_remote_copy(
            src_ref=recv.at[k, c, pl.ds(0, slab - 1), planes],
            dst_ref=recv.at[k, c, pl.ds(0, slab - 1), planes],
            send_sem=send_sem.at[k],
            recv_sem=arrived,
            device_id={"slab": lax.rem(me_s + 1, slab)},
            device_id_type=MESH,
        )

    def all_sent(k):
        return pltpu.make_async_remote_copy(
            src_ref=send.at[k, :, pl.ds(0, slab - 1)],
            dst_ref=recv.at[k, :, pl.ds(0, slab - 1)],
            send_sem=send_sem.at[k],
            recv_sem=recv_sem.at[k, 0],
            device_id={"slab": lax.rem(me_s + 1, slab)},
            device_id_type=MESH,
        )

    def own_copy(k, c):
        return pltpu.make_async_copy(send.at[k, c, me_s], recv.at[k, c, me_s], own_sem.at[k, c])

    lane = lax.broadcasted_iota(jnp.int32, (ROWS, LANES), 1)

    def rows_pass(k, c, first, planes):
        lefts = []
        for i in range(slab):
            pieces = []
            for part in range(2):
                at = (part * coils + c) * slab + i
                for j in range(ny // LANES):
                    pieces.append(grid[j, pl.ds(first * rows + at, planes, stride=rows), :])
            lefts.append(jnp.concatenate(pieces, axis=1))
        hybrid = jnp.dot(
            jnp.concatenate(lefts, axis=0).astype(jnp.bfloat16),
            ky_tab[...],
            preferred_element_type=jnp.float32,
        )
        turned = []
        for part in range(2):
            values = []
            for i in range(slab):
                value = hybrid[i * planes : (i + 1) * planes, part * ny : (part + 1) * ny]
                values.append(pltpu.roll(value, i * yb, 1) if i else value)
            turned.append(values)
        for d in range(slab):
            for j in range(ny // LANES):
                low, high = j * LANES // yb, ((j + 1) * LANES - 1) // yb
                cut = slice(j * LANES, (j + 1) * LANES)
                parts = []
                for values in turned:
                    tile = values[(low - d) % slab][:, cut]
                    for p in range(low + 1, high + 1):
                        tile = jnp.where(
                            lane[:planes] >= p * yb - j * LANES, values[(p - d) % slab][:, cut], tile
                        )
                    parts.append(tile)
                for g in range(planes // HALF):
                    both = [tile[g * HALF : (g + 1) * HALF] for tile in parts]
                    send[k, c, d, lax.div(first, HALF) + g, :, cut] = jnp.concatenate(
                        both, axis=0
                    ).astype(jnp.bfloat16)

    def send_rows(k, c, first, planes):
        for d in across(me_s, slab) + beside(me_s, slab):
            block_copy(k, first, planes, c, d, recv_sem.at[k, c]).start()

    def fill(k, b):
        load_k(k, b).wait()
        lax.fori_loop(0, slab, functools.partial(unpack, chunk_of(k) * slab, b), 0)

    def later_loads():
        for j in range(blocks, chunks * blocks):
            load_k(jnp.int32(j // blocks), j % blocks).start()
        load_m.start()
        load_z.start()

    def block_pass(j, carry):
        k, b = lax.div(j, blocks), lax.rem(j, blocks)
        first = pl.multiple_of(b * ROWS, ROWS)
        fill(k, b)
        lax.fori_loop(0, count, functools.partial(place, first), 0, unroll=UNROLL)
        if not split:

            @pl.when(j == 0)
            def _():
                load_y.wait()

        def one_coil(c, inner):
            rows_pass(k, c, first, ROWS)

            @pl.when(((k == 0) & (last > 0)) | ((k == last) & (b < woven)))
            def _():
                send_rows(k, c, first, ROWS)

            @pl.when(b == blocks - 1)
            def _():
                own_copy(k, c).start()

            return inner

        if not split:

            @pl.when(j == 0)
            def _():
                pl.semaphore_wait(barrier, slab + coil - 2)
                later_loads()

        lax.fori_loop(0, coils, one_coil, 0)

        @pl.when((k > 0) & (k < last) & (b == blocks - 1))
        def _():
            for d in across(me_s, slab) + beside(me_s, slab):
                for c in range(coils):
                    block_copy(k, 0, kzp, c, d, recv_sem.at[k, c]).start()

        return carry

    def half_pass(q, carry):
        first = pl.multiple_of(lax.div(q, coils) * HALF, HALF)
        c = lax.rem(q, coils)

        @pl.when(c == 0)
        def _():
            lax.fori_loop(0, HALF, functools.partial(place, first), 0, unroll=HALF)

        @pl.when(q == 0)
        def _():
            load_y.wait()

        rows_pass(0, c, first, HALF)

        @pl.when(q == 0)
        def _():
            pl.semaphore_wait(barrier, slab + coil - 2)

        send_rows(0, c, first, HALF)
        return carry

    load_i.wait()
    if split:
        fill(jnp.int32(0), 0)
        lax.fori_loop(0, coils * (ROWS // HALF), half_pass, 0)
        later_loads()
        if blocks == 1:
            for c in range(coils):
                own_copy(0, c).start()
    lax.fori_loop(int(split), chunks * blocks, block_pass, 0)
    far, near = across(me_s, slab), beside(me_s, slab)
    middle = len(far) // 2
    ends = range(woven, blocks)
    order = [(d, b) for d in far[:middle] + near for b in ends]
    order += [(d, b) for b in ends for d in far[middle:]]
    for d, b in order:
        for c in range(coils):
            arrived = recv_sem.at[last, c] if b < blocks - 1 else last_sem.at[c]
            block_copy(last, b * ROWS, ROWS, c, d, arrived).start()
    load_m.wait()
    load_z.wait()

    def part_copy(k, q):
        owner = chunk_of(k) * owners + q
        return pltpu.make_async_remote_copy(
            src_ref=part_send.at[chunk_of(k), pl.ds(q * xo, xo)],
            dst_ref=part_recv.at[lax.rem(owner - me_c + coil, coil)],
            send_sem=psend_sem.at[k, q],
            recv_sem=precv_sem.at[lax.rem(owner - me_c + coil, coil)],
            device_id={"coil": owner},
            device_id_type=MESH,
        )

    def depth(k, c, at, planes):
        block = recv[k, c, :, tiles(at, planes)].reshape(slab * 2 * planes, slab * yb)
        table = kz_tab[:, tiles(at, planes)].reshape(slab * 2 * planes, 2 * nz)
        return lax.dot_general(
            block, table, (((0,), (0,)), ((), ())), preferred_element_type=jnp.float32
        )

    def combined(c, p, x):
        real = image[c, pl.ds(p * yb, yb), :nz]
        imag = image[c, pl.ds(p * yb, yb), nz:]
        map_real = maps[0, c, x].astype(jnp.float32)
        map_imag = maps[1, c, x].astype(jnp.float32)
        return map_real * real + map_imag * imag, map_real * imag - map_imag * real

    def depth_pass(k, carry):
        first = chunk_of(k) * slab

        def one_coil(c, inner):
            own_copy(k, c).wait()
            @pl.when(k < last)
            def _():
                all_of(k, c, tiles(0, kzp), recv_sem.at[k, c]).wait_recv()

            image[c] = depth(k, c, 0, kzp)
            return inner

        lax.fori_loop(0, coils, one_coil, 0)
        for p in range(slab):
            x = lax.rem(p - me_s + slab, slab)
            add_real, add_imag = combined(0, p, first + x)
            for c in range(1, coils):
                term_real, term_imag = combined(c, p, first + x)
                add_real, add_imag = add_real + term_real, add_imag + term_imag
            part_send[chunk_of(k), x, 0] = add_real.astype(jnp.bfloat16)
            part_send[chunk_of(k), x, 1] = add_imag.astype(jnp.bfloat16)
        for q in range(owners):
            @pl.when(chunk_of(k) * owners + q != me_c)
            def _():
                part_copy(k, q).start()
        return carry

    def wait_parts():
        for o in range(1, coil):
            pltpu.make_async_remote_copy(
                src_ref=part_recv.at[o],
                dst_ref=part_recv.at[o],
                send_sem=psend_sem.at[0, 0],
                recv_sem=precv_sem.at[o],
                device_id={"coil": lax.rem(me_c + o, coil)},
                device_id_type=MESH,
            ).wait_recv()

    def drain(k, carry):
        all_sent(k).wait_send()
        for q in range(owners):
            @pl.when(chunk_of(k) * owners + q != me_c)
            def _():
                part_copy(k, q).wait_send()
        return carry

    own_chunk = lax.div(me_c, owners)

    if owners == 1 and coil > 1:
        lax.fori_loop(0, last, depth_pass, 0)
        wait_parts()

        def add_up(c):
            for p in range(slab):
                x = lax.rem(p - me_s + slab, slab)
                add_real, add_imag = combined(c, p, own_chunk * slab + x)
                out_ref[x, 0] += add_real
                out_ref[x, 1] += add_imag

        def total(i, carry):
            value = part_recv[1, i].astype(jnp.float32)
            for o in range(2, coil):
                value = value + part_recv[o, i].astype(jnp.float32)
            out_ref[i] = value
            return carry

        lax.fori_loop(0, xo, total, 0)
        for c in range(coils):
            own_copy(last, c).wait()
        if blocks > 1:
            for c in range(coils):
                all_of(last, c, tiles(0, early), recv_sem.at[last, c]).wait_recv()
                image[c] = depth(last, c, 0, early)
            for c in range(coils):
                add_up(c)
        lax.fori_loop(0, last, drain, 0)
        final = coils - 1
        for p in range(slab):
            x = own_chunk * slab + lax.rem(p - me_s + slab, slab)
            for part in range(2):
                held_maps[part, p] = maps[part, final, x]
        held_table[...] = kz_tab[:, tiles(early, ROWS)]
        for c in range(final):
            all_of(last, c, tiles(early, ROWS), last_sem.at[c]).wait_recv()
            image[c] = depth(last, c, early, ROWS)
            add_up(c)
        all_of(last, final, tiles(early, ROWS), last_sem.at[final]).wait_recv()
        block_ref[...] = recv[last, final, :, tiles(early, ROWS)]
        drain(last, 0)
    else:

        lax.fori_loop(0, last, depth_pass, 0)
        for c in range(coils):
            if blocks > 1:
                all_of(last, c, tiles(0, early), recv_sem.at[last, c]).wait_recv()
            all_of(last, c, tiles(early, ROWS), last_sem.at[c]).wait_recv()
        depth_pass(last, 0)
        wait_parts()
        own_at = lax.rem(me_c, owners) * xo

        def total(i, carry):
            value = part_send[own_chunk, own_at + i].astype(jnp.float32)
            for o in range(1, coil):
                value = value + part_recv[o, i].astype(jnp.float32)
            out_ref[i] = value
            return carry

        lax.fori_loop(0, xo, total, 0)
        lax.fori_loop(0, chunks, drain, 0)
        for unused in (block_ref, held_maps, held_table):
            unused[...] = jnp.zeros_like(unused)


def finish(slab, out_ref_in, block_ref, held_maps, held_table, out_ref, image, stage, sem):
    me_s = lax.axis_index("slab")
    yb, nz = stage.shape[2:]
    ny = slab * yb
    depth = block_ref.shape[0] * block_ref.shape[1] * block_ref.shape[2]
    table = held_table[...].reshape(depth, 2 * nz)
    copies = []
    for j in range(ny // LANES):
        low, high = j * LANES, (j + 1) * LANES
        image[low:high] = lax.dot_general(
            block_ref[:, :, :, low:high].reshape(depth, LANES),
            table,
            (((0,), (0,)), ((), ())),
            preferred_element_type=jnp.float32,
        )
        for p in range(low // yb, high // yb):
            x = lax.rem(p - me_s + slab, slab)
            real = image[p * yb : (p + 1) * yb, :nz]
            imag = image[p * yb : (p + 1) * yb, nz:]
            map_real = held_maps[0, p].astype(jnp.float32)
            map_imag = held_maps[1, p].astype(jnp.float32)
            stage[p, 0] = out_ref_in[x, 0] + (map_real * real + map_imag * imag)
            stage[p, 1] = out_ref_in[x, 1] + (map_real * imag - map_imag * real)
            copies.append(pltpu.make_async_copy(stage.at[p], out_ref.at[x], sem.at[p]))
            copies[-1].start()
    for copy in copies:
        copy.wait()


def local(mesh, kspace, coil_maps, line_index):
    slab, coil = mesh.shape["slab"], mesh.shape["coil"]
    _, coils, offs, xr, kzb, lines = kspace.shape
    yb, nz = coil_maps.shape[3:]
    ny = yb * slab
    kzp = up(kzb, 16)
    dims = (slab, coil, coils, offs, xr, kzb, kzp, lines, ny, yb, nz)
    chunks, xo = xr // slab, xr // coil
    owners = slab // xo
    rows = 2 * coils * slab
    f32, bf16 = jnp.float32, jnp.bfloat16

    ky_table = np.concatenate(dense_table(np.arange(ny), np.ones(ny), ny), 0)
    local_kz = np.arange(kzp)
    per_slab = []
    for s in range(slab):
        per_slab += dense_table(s * kzb + local_kz, (local_kz < kzb) * 1.0, nz)
    kz_table = np.concatenate(per_slab, 0).reshape(slab, 2, kzp // HALF, HALF, 2 * nz)
    kz_table = kz_table.swapaxes(1, 2).reshape(slab, kzp // HALF, 2 * HALF, 2 * nz)
    ky_table = jnp.asarray(ky_table.astype(np.float32)).astype(bf16)
    kz_table = jnp.asarray(kz_table.astype(np.float32)).astype(bf16)

    vmem, hbm = pl.BlockSpec(memory_space=pltpu.VMEM), pl.BlockSpec(memory_space=pltpu.HBM)
    dma = pltpu.SemaphoreType.DMA
    direct = owners == 1 and coil > 1
    small = (lambda *shape: shape) if direct else (lambda *shape: (8, 128))
    result = pl.pallas_call(
        functools.partial(kernel, dims),
        out_shape=[
            jax.ShapeDtypeStruct((xo, 2, yb, nz), f32),
            jax.ShapeDtypeStruct(small(slab, ROWS // HALF, 2 * HALF, ny), bf16),
            jax.ShapeDtypeStruct(small(2, slab, yb, nz), bf16),
            jax.ShapeDtypeStruct(small(slab, ROWS // HALF, 2 * HALF, 2 * nz), bf16),
        ],
        in_specs=[hbm] * 5,
        out_specs=[vmem] * 4,
        scratch_shapes=[
            pltpu.VMEM(kspace.shape, bf16),
            pltpu.VMEM(line_index.shape, jnp.int32),
            pltpu.VMEM((offs, rows * up(kzb, 8), lines), f32),
            pltpu.VMEM((ny // LANES, kzp * rows, LANES), f32),
            pltpu.VMEM(coil_maps.shape, bf16),
            pltpu.VMEM(ky_table.shape, bf16),
            pltpu.VMEM(kz_table.shape, bf16),
            pltpu.VMEM((chunks, coils, slab, kzp // HALF, 2 * HALF, ny), bf16),
            pltpu.VMEM((chunks, coils, slab, kzp // HALF, 2 * HALF, ny), bf16),
            pltpu.VMEM((coils, ny, 2 * nz), f32),
            pltpu.VMEM((chunks, slab, 2, yb, nz), bf16),
            pltpu.VMEM((coil, xo, 2, yb, nz), bf16),
            dma((4,)),
            dma((chunks, kzp // ROWS)),
            dma((chunks,)),
            dma((chunks, coils)),
            dma((coils,)),
            dma((chunks, coils)),
            dma((chunks, owners)),
            dma((coil,)),
        ],
        compiler_params=pltpu.CompilerParams(
            collective_id=0, has_side_effects=True, vmem_limit_bytes=VLIM * 1024 * 1024
        ),
    )(
        *(
            pltpu.with_memory_space_constraint(operand, pltpu.HBM)
            for operand in (kspace, coil_maps, line_index, ky_table, kz_table)
        )
    )
    if not direct:
        return result[0]
    return pl.pallas_call(
        functools.partial(finish, slab),
        out_shape=jax.ShapeDtypeStruct((xo, 2, yb, nz), f32),
        in_specs=[vmem] * 4,
        out_specs=hbm,
        scratch_shapes=[
            pltpu.VMEM((ny, 2 * nz), f32),
            pltpu.VMEM((xo, 2, yb, nz), f32),
            dma((xo,)),
        ],
        compiler_params=pltpu.CompilerParams(vmem_limit_bytes=FINISH * 1024 * 1024),
    )(*result)


def solution(mesh):
    placed = (
        P(None, "coil", None, None, "slab", None),
        P(None, "coil", None, "slab", None),
        P(None, "slab", None),
    )
    return jax.shard_map(
        functools.partial(local, mesh),
        mesh=mesh,
        in_specs=placed,
        out_specs=P("coil", None, "slab", None),
        check_vma=False,
    )
```

```python
import functools
import math

import jax
import jax.numpy as jnp
import numpy as np
from jax import lax
from jax.experimental import pallas as pl
from jax.experimental.pallas import tpu as pltpu
from jax.sharding import PartitionSpec as P

PHASES = 8
LANES = 128
UNROLL = 16
VLIM = 48
FINISH = 8
ROWS = 16
HALF = 8
MESH = pl.DeviceIdType.MESH


def across(me, slab):
    half = slab // 2
    other = half - lax.div(me, half) * half
    return [other + i for i in range(half)]


def beside(me, slab):
    half = slab // 2
    first = lax.div(me, half) * half
    return [first + lax.rem(me + i, half) for i in range(1, half)]


def up(value, unit):
    return -(-value // unit) * unit


def dense_table(rows, row_ok, length):
    turns = rows[:, None].astype(np.int64) * np.arange(length)[None, :] % length
    angles = turns.astype(np.float64) * (2.0 * math.pi / length)
    scaling = row_ok[:, None] / math.sqrt(length)
    cos, sin = np.cos(angles) * scaling, np.sin(angles) * scaling
    return np.concatenate([cos, sin], 1), np.concatenate([-sin, cos], 1)


def kernel(
    dims,
    kspace_ref, maps_ref, index_ref, ky_ref, kz_ref, out_ref, block_ref, held_maps, held_table,
    raw, index, samples, grid, maps, ky_tab, kz_tab, send, recv, image, part_send, part_recv,
    in_sem, load_sem, send_sem, recv_sem, last_sem, own_sem, psend_sem, precv_sem,
):
    slab, coil, coils, offs, xr, kzb, kzp, lines, ny, yb, nz = dims
    me_s, me_c = lax.axis_index("slab"), lax.axis_index("coil")
    rows = 2 * coils * slab
    kzs = up(kzb, 8)
    chunks = xr // slab
    last = chunks - 1
    xo = xr // coil
    owners = slab // xo
    blocks = kzp // ROWS
    early = (blocks - 1) * ROWS
    woven = max(blocks - 2, 0)
    split = last > 0 and kzb % ROWS == 0

    barrier = pltpu.get_barrier_semaphore()
    for d in across(me_s, slab) + beside(me_s, slab):
        pl.semaphore_signal(barrier, inc=1, device_id={"slab": d}, device_id_type=MESH)
    for o in range(1, coil):
        pl.semaphore_signal(
            barrier, inc=1, device_id={"coil": lax.rem(me_c + o, coil)}, device_id_type=MESH
        )

    def chunk_of(k):
        own = lax.div(me_c, owners)
        if chunks % 2:
            return lax.rem(own + 1 + k, chunks)
        pair = lax.rem(lax.div(own, 2) + 1 + lax.div(k, 2), chunks // 2)
        return 2 * pair + lax.rem(own + 1 + k, 2)

    count = min(ROWS, kzb)

    def load_k(k, b):
        at = pl.ds(chunk_of(k) * slab, slab)
        planes = pl.ds(b * ROWS, count)
        return pltpu.make_async_copy(
            kspace_ref.at[:, :, :, at, planes], raw.at[:, :, :, at, planes], load_sem.at[k, b]
        )

    load_i = pltpu.make_async_copy(index_ref, index, in_sem.at[3])
    load_m = pltpu.make_async_copy(maps_ref, maps, in_sem.at[0])
    load_y = pltpu.make_async_copy(ky_ref, ky_tab, in_sem.at[1])
    load_z = pltpu.make_async_copy(kz_ref, kz_tab, in_sem.at[2])
    load_k(jnp.int32(0), 0).start()
    load_i.start()
    load_y.start()
    for b in range(1, blocks):
        load_k(jnp.int32(0), b).start()

    if kzp != kzb:
        grid[...] = jnp.zeros_like(grid)

    def unpack(first, b, i, carry):
        kz_at = pl.multiple_of(b * ROWS, ROWS)
        for c in range(coils):
            for t in range(offs):
                angle = 2.0 * math.pi * t / PHASES
                real = raw[0, c, t, first + i, pl.ds(kz_at, count)].astype(jnp.float32)
                imag = raw[1, c, t, first + i, pl.ds(kz_at, count)].astype(jnp.float32)
                if t:
                    cosine, sine = math.cos(angle), math.sin(angle)
                    real, imag = cosine * real + sine * imag, cosine * imag - sine * real
                for part, value in ((0, real), (1, imag)):
                    at = pl.multiple_of(((part * coils + c) * slab + i) * kzs + kz_at, 8)
                    samples[t, pl.ds(at, count), :] = value
        return carry

    ky_at = lax.broadcasted_iota(jnp.int32, (ny, offs * lines), 0)

    def place(first_kz, step, carry):
        kz = first_kz + step
        picked = jnp.concatenate([index[t, pl.ds(kz, 1), :] for t in range(offs)], axis=1)
        hot = jnp.where(ky_at == picked, 1.0, 0.0).astype(jnp.bfloat16)
        left = jnp.concatenate(
            [samples[t, pl.ds(kz, rows, stride=kzs), :].astype(jnp.bfloat16) for t in range(offs)],
            axis=1,
        )
        grid_at = pl.multiple_of(kz * rows, 8)
        placed = lax.dot_general(
            left, hot, (((1,), (1,)), ((), ())), preferred_element_type=jnp.float32
        )
        for j in range(ny // LANES):
            grid[j, pl.ds(grid_at, rows), :] = placed[:, j * LANES : (j + 1) * LANES]
        return carry


    def tiles(first, planes):
        return pl.ds(lax.div(first, HALF), planes // HALF)

    def block_copy(k, first, planes, c, d, arrived):
        return pltpu.make_async_remote_copy(
            src_ref=send.at[k, c, d, tiles(first, planes)],
            dst_ref=recv.at[k, c, me_s, tiles(first, planes)],
            send_sem=send_sem.at[k],
            recv_sem=arrived,
            device_id={"slab": d},
            device_id_type=MESH,
        )

    def all_of(k, c, planes, arrived):
        return pltpu.make_async_remote_copy(
            src_ref=recv.at[k, c, pl.ds(0, slab - 1), planes],
            dst_ref=recv.at[k, c, pl.ds(0, slab - 1), planes],
            send_sem=send_sem.at[k],
            recv_sem=arrived,
            device_id={"slab": lax.rem(me_s + 1, slab)},
            device_id_type=MESH,
        )

    def all_sent(k):
        return pltpu.make_async_remote_copy(
            src_ref=send.at[k, :, pl.ds(0, slab - 1)],
            dst_ref=recv.at[k, :, pl.ds(0, slab - 1)],
            send_sem=send_sem.at[k],
            recv_sem=recv_sem.at[k, 0],
            device_id={"slab": lax.rem(me_s + 1, slab)},
            device_id_type=MESH,
        )

    def own_copy(k, c):
        return pltpu.make_async_copy(send.at[k, c, me_s], recv.at[k, c, me_s], own_sem.at[k, c])

    lane = lax.broadcasted_iota(jnp.int32, (ROWS, LANES), 1)

    def rows_pass(k, c, first, planes):
        lefts = []
        for i in range(slab):
            pieces = []
            for part in range(2):
                at = (part * coils + c) * slab + i
                for j in range(ny // LANES):
                    pieces.append(grid[j, pl.ds(first * rows + at, planes, stride=rows), :])
            lefts.append(jnp.concatenate(pieces, axis=1))
        hybrid = jnp.dot(
            jnp.concatenate(lefts, axis=0).astype(jnp.bfloat16),
            ky_tab[...],
            preferred_element_type=jnp.float32,
        )
        turned = []
        for part in range(2):
            values = []
            for i in range(slab):
                value = hybrid[i * planes : (i + 1) * planes, part * ny : (part + 1) * ny]
                values.append(pltpu.roll(value, i * yb, 1) if i else value)
            turned.append(values)
        for d in range(slab):
            for j in range(ny // LANES):
                low, high = j * LANES // yb, ((j + 1) * LANES - 1) // yb
                cut = slice(j * LANES, (j + 1) * LANES)
                parts = []
                for values in turned:
                    tile = values[(low - d) % slab][:, cut]
                    for p in range(low + 1, high + 1):
                        tile = jnp.where(
                            lane[:planes] >= p * yb - j * LANES, values[(p - d) % slab][:, cut], tile
                        )
                    parts.append(tile)
                for g in range(planes // HALF):
                    both = [tile[g * HALF : (g + 1) * HALF] for tile in parts]
                    send[k, c, d, lax.div(first, HALF) + g, :, cut] = jnp.concatenate(
                        both, axis=0
                    ).astype(jnp.bfloat16)

    def send_rows(k, c, first, planes):
        for d in across(me_s, slab) + beside(me_s, slab):
            block_copy(k, first, planes, c, d, recv_sem.at[k, c]).start()

    def fill(k, b):
        load_k(k, b).wait()
        lax.fori_loop(0, slab, functools.partial(unpack, chunk_of(k) * slab, b), 0)

    def later_loads():
        for j in range(blocks, chunks * blocks):
            load_k(jnp.int32(j // blocks), j % blocks).start()
        load_m.start()
        load_z.start()

    def block_pass(j, carry):
        k, b = lax.div(j, blocks), lax.rem(j, blocks)
        first = pl.multiple_of(b * ROWS, ROWS)
        fill(k, b)
        lax.fori_loop(0, count, functools.partial(place, first), 0, unroll=UNROLL)
        if not split:

            @pl.when(j == 0)
            def _():
                load_y.wait()

        def one_coil(c, inner):
            rows_pass(k, c, first, ROWS)

            @pl.when(((k == 0) & (last > 0)) | ((k == last) & (b < woven)))
            def _():
                send_rows(k, c, first, ROWS)

            @pl.when(b == blocks - 1)
            def _():
                own_copy(k, c).start()

            return inner

        if not split:

            @pl.when(j == 0)
            def _():
                pl.semaphore_wait(barrier, slab + coil - 2)
                later_loads()

        lax.fori_loop(0, coils, one_coil, 0)

        @pl.when((k > 0) & (k < last) & (b == blocks - 1))
        def _():
            for d in across(me_s, slab) + beside(me_s, slab):
                for c in range(coils):
                    block_copy(k, 0, kzp, c, d, recv_sem.at[k, c]).start()

        return carry

    def half_pass(q, carry):
        first = pl.multiple_of(lax.div(q, coils) * HALF, HALF)
        c = lax.rem(q, coils)

        @pl.when(c == 0)
        def _():
            lax.fori_loop(0, HALF, functools.partial(place, first), 0, unroll=HALF)

        @pl.when(q == 0)
        def _():
            load_y.wait()

        rows_pass(0, c, first, HALF)

        @pl.when(q == 0)
        def _():
            pl.semaphore_wait(barrier, slab + coil - 2)

        send_rows(0, c, first, HALF)
        return carry

    load_i.wait()
    if split:
        fill(jnp.int32(0), 0)
        lax.fori_loop(0, coils * (ROWS // HALF), half_pass, 0)
        later_loads()
        if blocks == 1:
            for c in range(coils):
                own_copy(0, c).start()
    lax.fori_loop(int(split), chunks * blocks, block_pass, 0)
    far, near = across(me_s, slab), beside(me_s, slab)
    middle = len(far) // 2
    ends = range(woven, blocks)
    order = [(d, b) for d in far[:middle] + near for b in ends]
    order += [(d, b) for b in ends for d in far[middle:]]
    for d, b in order:
        for c in range(coils):
            arrived = recv_sem.at[last, c] if b < blocks - 1 else last_sem.at[c]
            block_copy(last, b * ROWS, ROWS, c, d, arrived).start()
    load_m.wait()
    load_z.wait()

    def part_copy(k, q):
        owner = chunk_of(k) * owners + q
        return pltpu.make_async_remote_copy(
            src_ref=part_send.at[chunk_of(k), pl.ds(q * xo, xo)],
            dst_ref=part_recv.at[lax.rem(owner - me_c + coil, coil)],
            send_sem=psend_sem.at[k, q],
            recv_sem=precv_sem.at[lax.rem(owner - me_c + coil, coil)],
            device_id={"coil": owner},
            device_id_type=MESH,
        )

    def depth(k, c, at, planes):
        block = recv[k, c, :, tiles(at, planes)].reshape(slab * 2 * planes, slab * yb)
        table = kz_tab[:, tiles(at, planes)].reshape(slab * 2 * planes, 2 * nz)
        return lax.dot_general(
            block, table, (((0,), (0,)), ((), ())), preferred_element_type=jnp.float32
        )

    def combined(c, p, x):
        real = image[c, pl.ds(p * yb, yb), :nz]
        imag = image[c, pl.ds(p * yb, yb), nz:]
        map_real = maps[0, c, x].astype(jnp.float32)
        map_imag = maps[1, c, x].astype(jnp.float32)
        return map_real * real + map_imag * imag, map_real * imag - map_imag * real

    def depth_pass(k, carry):
        first = chunk_of(k) * slab

        def one_coil(c, inner):
            own_copy(k, c).wait()
            @pl.when(k < last)
            def _():
                all_of(k, c, tiles(0, kzp), recv_sem.at[k, c]).wait_recv()

            image[c] = depth(k, c, 0, kzp)
            return inner

        lax.fori_loop(0, coils, one_coil, 0)
        for p in range(slab):
            x = lax.rem(p - me_s + slab, slab)
            add_real, add_imag = combined(0, p, first + x)
            for c in range(1, coils):
                term_real, term_imag = combined(c, p, first + x)
                add_real, add_imag = add_real + term_real, add_imag + term_imag
            part_send[chunk_of(k), x, 0] = add_real.astype(jnp.bfloat16)
            part_send[chunk_of(k), x, 1] = add_imag.astype(jnp.bfloat16)
        for q in range(owners):
            @pl.when(chunk_of(k) * owners + q != me_c)
            def _():
                part_copy(k, q).start()
        return carry

    def wait_parts():
        for o in range(1, coil):
            pltpu.make_async_remote_copy(
                src_ref=part_recv.at[o],
                dst_ref=part_recv.at[o],
                send_sem=psend_sem.at[0, 0],
                recv_sem=precv_sem.at[o],
                device_id={"coil": lax.rem(me_c + o, coil)},
                device_id_type=MESH,
            ).wait_recv()

    def drain(k, carry):
        all_sent(k).wait_send()
        for q in range(owners):
            @pl.when(chunk_of(k) * owners + q != me_c)
            def _():
                part_copy(k, q).wait_send()
        return carry

    own_chunk = lax.div(me_c, owners)

    if owners == 1 and coil > 1:
        lax.fori_loop(0, last, depth_pass, 0)
        wait_parts()

        def add_up(c):
            for p in range(slab):
                x = lax.rem(p - me_s + slab, slab)
                add_real, add_imag = combined(c, p, own_chunk * slab + x)
                out_ref[x, 0] += add_real
                out_ref[x, 1] += add_imag

        def total(i, carry):
            value = part_recv[1, i].astype(jnp.float32)
            for o in range(2, coil):
                value = value + part_recv[o, i].astype(jnp.float32)
            out_ref[i] = value
            return carry

        lax.fori_loop(0, xo, total, 0)
        for c in range(coils):
            own_copy(last, c).wait()
        if blocks > 1:
            for c in range(coils):
                all_of(last, c, tiles(0, early), recv_sem.at[last, c]).wait_recv()
                image[c] = depth(last, c, 0, early)
            for c in range(coils):
                add_up(c)
        lax.fori_loop(0, last, drain, 0)
        final = coils - 1
        for p in range(slab):
            x = own_chunk * slab + lax.rem(p - me_s + slab, slab)
            for part in range(2):
                held_maps[part, p] = maps[part, final, x]
        held_table[...] = kz_tab[:, tiles(early, ROWS)]
        for c in range(final):
            all_of(last, c, tiles(early, ROWS), last_sem.at[c]).wait_recv()
            image[c] = depth(last, c, early, ROWS)
            add_up(c)
        all_of(last, final, tiles(early, ROWS), last_sem.at[final]).wait_recv()
        block_ref[...] = recv[last, final, :, tiles(early, ROWS)]
        drain(last, 0)
    else:

        lax.fori_loop(0, last, depth_pass, 0)
        for c in range(coils):
            if blocks > 1:
                all_of(last, c, tiles(0, early), recv_sem.at[last, c]).wait_recv()
            all_of(last, c, tiles(early, ROWS), last_sem.at[c]).wait_recv()
        depth_pass(last, 0)
        wait_parts()
        own_at = lax.rem(me_c, owners) * xo

        def total(i, carry):
            value = part_send[own_chunk, own_at + i].astype(jnp.float32)
            for o in range(1, coil):
                value = value + part_recv[o, i].astype(jnp.float32)
            out_ref[i] = value
            return carry

        lax.fori_loop(0, xo, total, 0)
        lax.fori_loop(0, chunks, drain, 0)
        for unused in (block_ref, held_maps, held_table):
            unused[...] = jnp.zeros_like(unused)


def finish(slab, out_ref_in, block_ref, held_maps, held_table, out_ref, image, stage, sem):
    me_s = lax.axis_index("slab")
    yb, nz = stage.shape[2:]
    ny = slab * yb
    depth = block_ref.shape[0] * block_ref.shape[1] * block_ref.shape[2]
    table = held_table[...].reshape(depth, 2 * nz)
    image[...] = lax.dot_general(
        block_ref[...].reshape(depth, ny),
        table,
        (((0,), (0,)), ((), ())),
        preferred_element_type=jnp.float32,
    )
    copies = []
    for p in range(slab):
        x = lax.rem(p - me_s + slab, slab)
        real = image[p * yb : (p + 1) * yb, :nz]
        imag = image[p * yb : (p + 1) * yb, nz:]
        map_real = held_maps[0, p].astype(jnp.float32)
        map_imag = held_maps[1, p].astype(jnp.float32)
        stage[p, 0] = out_ref_in[x, 0] + (map_real * real + map_imag * imag)
        stage[p, 1] = out_ref_in[x, 1] + (map_real * imag - map_imag * real)
        copies.append(pltpu.make_async_copy(stage.at[p], out_ref.at[x], sem.at[p]))
        copies[-1].start()
    for copy in copies:
        copy.wait()


def local(mesh, kspace, coil_maps, line_index):
    slab, coil = mesh.shape["slab"], mesh.shape["coil"]
    _, coils, offs, xr, kzb, lines = kspace.shape
    yb, nz = coil_maps.shape[3:]
    ny = yb * slab
    kzp = up(kzb, 16)
    dims = (slab, coil, coils, offs, xr, kzb, kzp, lines, ny, yb, nz)
    chunks, xo = xr // slab, xr // coil
    owners = slab // xo
    rows = 2 * coils * slab
    f32, bf16 = jnp.float32, jnp.bfloat16

    ky_table = np.concatenate(dense_table(np.arange(ny), np.ones(ny), ny), 0)
    local_kz = np.arange(kzp)
    per_slab = []
    for s in range(slab):
        per_slab += dense_table(s * kzb + local_kz, (local_kz < kzb) * 1.0, nz)
    kz_table = np.concatenate(per_slab, 0).reshape(slab, 2, kzp // HALF, HALF, 2 * nz)
    kz_table = kz_table.swapaxes(1, 2).reshape(slab, kzp // HALF, 2 * HALF, 2 * nz)
    ky_table = jnp.asarray(ky_table.astype(np.float32)).astype(bf16)
    kz_table = jnp.asarray(kz_table.astype(np.float32)).astype(bf16)

    vmem, hbm = pl.BlockSpec(memory_space=pltpu.VMEM), pl.BlockSpec(memory_space=pltpu.HBM)
    dma = pltpu.SemaphoreType.DMA
    direct = owners == 1 and coil > 1
    small = (lambda *shape: shape) if direct else (lambda *shape: (8, 128))
    result = pl.pallas_call(
        functools.partial(kernel, dims),
        out_shape=[
            jax.ShapeDtypeStruct((xo, 2, yb, nz), f32),
            jax.ShapeDtypeStruct(small(slab, ROWS // HALF, 2 * HALF, ny), bf16),
            jax.ShapeDtypeStruct(small(2, slab, yb, nz), bf16),
            jax.ShapeDtypeStruct(small(slab, ROWS // HALF, 2 * HALF, 2 * nz), bf16),
        ],
        in_specs=[hbm] * 5,
        out_specs=[vmem] * 4,
        scratch_shapes=[
            pltpu.VMEM(kspace.shape, bf16),
            pltpu.VMEM(line_index.shape, jnp.int32),
            pltpu.VMEM((offs, rows * up(kzb, 8), lines), f32),
            pltpu.VMEM((ny // LANES, kzp * rows, LANES), f32),
            pltpu.VMEM(coil_maps.shape, bf16),
            pltpu.VMEM(ky_table.shape, bf16),
            pltpu.VMEM(kz_table.shape, bf16),
            pltpu.VMEM((chunks, coils, slab, kzp // HALF, 2 * HALF, ny), bf16),
            pltpu.VMEM((chunks, coils, slab, kzp // HALF, 2 * HALF, ny), bf16),
            pltpu.VMEM((coils, ny, 2 * nz), f32),
            pltpu.VMEM((chunks, slab, 2, yb, nz), bf16),
            pltpu.VMEM((coil, xo, 2, yb, nz), bf16),
            dma((4,)),
            dma((chunks, kzp // ROWS)),
            dma((chunks,)),
            dma((chunks, coils)),
            dma((coils,)),
            dma((chunks, coils)),
            dma((chunks, owners)),
            dma((coil,)),
        ],
        compiler_params=pltpu.CompilerParams(
            collective_id=0, has_side_effects=True, vmem_limit_bytes=VLIM * 1024 * 1024
        ),
    )(
        *(
            pltpu.with_memory_space_constraint(operand, pltpu.HBM)
            for operand in (kspace, coil_maps, line_index, ky_table, kz_table)
        )
    )
    if not direct:
        return result[0]
    return pl.pallas_call(
        functools.partial(finish, slab),
        out_shape=jax.ShapeDtypeStruct((xo, 2, yb, nz), f32),
        in_specs=[vmem] * 4,
        out_specs=hbm,
        scratch_shapes=[
            pltpu.VMEM((ny, 2 * nz), f32),
            pltpu.VMEM((xo, 2, yb, nz), f32),
            dma((xo,)),
        ],
        compiler_params=pltpu.CompilerParams(vmem_limit_bytes=FINISH * 1024 * 1024),
    )(*result)


def solution(mesh):
    placed = (
        P(None, "coil", None, None, "slab", None),
        P(None, "coil", None, "slab", None),
        P(None, "slab", None),
    )
    return jax.shard_map(
        functools.partial(local, mesh),
        mesh=mesh,
        in_specs=placed,
        out_specs=P("coil", None, "slab", None),
        check_vma=False,
    )
```

```python
import functools
import math

import jax
import jax.numpy as jnp
import numpy as np
from jax import lax
from jax.experimental import pallas as pl
from jax.experimental.pallas import tpu as pltpu
from jax.sharding import PartitionSpec as P

PHASES = 8
LANES = 128
UNROLL = 16
VLIM = 48
FINISH = 8
ROWS = 16
HALF = 8
MESH = pl.DeviceIdType.MESH


def across(me, slab):
    half = slab // 2
    other = half - lax.div(me, half) * half
    return [other + i for i in range(half)]


def beside(me, slab):
    half = slab // 2
    first = lax.div(me, half) * half
    return [first + lax.rem(me + i, half) for i in range(1, half)]


def up(value, unit):
    return -(-value // unit) * unit


def dense_table(rows, row_ok, length):
    turns = rows[:, None].astype(np.int64) * np.arange(length)[None, :] % length
    angles = turns.astype(np.float64) * (2.0 * math.pi / length)
    scaling = row_ok[:, None] / math.sqrt(length)
    cos, sin = np.cos(angles) * scaling, np.sin(angles) * scaling
    return np.concatenate([cos, sin], 1), np.concatenate([-sin, cos], 1)


def kernel(
    dims,
    kspace_ref, maps_ref, index_ref, ky_ref, kz_ref, out_ref, block_ref, held_maps, held_table,
    raw, index, samples, grid, maps, ky_tab, kz_tab, send, recv, image, part_send, part_recv,
    in_sem, load_sem, send_sem, recv_sem, last_sem, own_sem, psend_sem, precv_sem,
):
    slab, coil, coils, offs, xr, kzb, kzp, lines, ny, yb, nz = dims
    me_s, me_c = lax.axis_index("slab"), lax.axis_index("coil")
    rows = 2 * coils * slab
    kzs = up(kzb, 8)
    chunks = xr // slab
    last = chunks - 1
    xo = xr // coil
    owners = slab // xo
    blocks = kzp // ROWS
    early = (blocks - 1) * ROWS
    split = last > 0 and kzb % ROWS == 0

    barrier = pltpu.get_barrier_semaphore()
    for d in across(me_s, slab) + beside(me_s, slab):
        pl.semaphore_signal(barrier, inc=1, device_id={"slab": d}, device_id_type=MESH)
    for o in range(1, coil):
        pl.semaphore_signal(
            barrier, inc=1, device_id={"coil": lax.rem(me_c + o, coil)}, device_id_type=MESH
        )

    def chunk_of(k):
        own = lax.div(me_c, owners)
        if chunks % 2:
            return lax.rem(own + 1 + k, chunks)
        pair = lax.rem(lax.div(own, 2) + 1 + lax.div(k, 2), chunks // 2)
        return 2 * pair + lax.rem(own + 1 + k, 2)

    count = min(ROWS, kzb)

    def load_k(k, b):
        at = pl.ds(chunk_of(k) * slab, slab)
        planes = pl.ds(b * ROWS, count)
        return pltpu.make_async_copy(
            kspace_ref.at[:, :, :, at, planes], raw.at[:, :, :, at, planes], load_sem.at[k, b]
        )

    load_i = pltpu.make_async_copy(index_ref, index, in_sem.at[3])
    load_m = pltpu.make_async_copy(maps_ref, maps, in_sem.at[0])
    load_y = pltpu.make_async_copy(ky_ref, ky_tab, in_sem.at[1])
    load_z = pltpu.make_async_copy(kz_ref, kz_tab, in_sem.at[2])
    load_k(jnp.int32(0), 0).start()
    load_i.start()
    load_y.start()
    for b in range(1, blocks):
        load_k(jnp.int32(0), b).start()

    if kzp != kzb:
        grid[...] = jnp.zeros_like(grid)

    def unpack(first, b, i, carry):
        kz_at = pl.multiple_of(b * ROWS, ROWS)
        for c in range(coils):
            for t in range(offs):
                angle = 2.0 * math.pi * t / PHASES
                real = raw[0, c, t, first + i, pl.ds(kz_at, count)].astype(jnp.float32)
                imag = raw[1, c, t, first + i, pl.ds(kz_at, count)].astype(jnp.float32)
                if t:
                    cosine, sine = math.cos(angle), math.sin(angle)
                    real, imag = cosine * real + sine * imag, cosine * imag - sine * real
                for part, value in ((0, real), (1, imag)):
                    at = pl.multiple_of(((part * coils + c) * slab + i) * kzs + kz_at, 8)
                    samples[t, pl.ds(at, count), :] = value
        return carry

    ky_at = lax.broadcasted_iota(jnp.int32, (ny, offs * lines), 0)

    def place(first_kz, step, carry):
        kz = first_kz + step
        picked = jnp.concatenate([index[t, pl.ds(kz, 1), :] for t in range(offs)], axis=1)
        hot = jnp.where(ky_at == picked, 1.0, 0.0).astype(jnp.bfloat16)
        left = jnp.concatenate(
            [samples[t, pl.ds(kz, rows, stride=kzs), :].astype(jnp.bfloat16) for t in range(offs)],
            axis=1,
        )
        grid_at = pl.multiple_of(kz * rows, 8)
        placed = lax.dot_general(
            left, hot, (((1,), (1,)), ((), ())), preferred_element_type=jnp.float32
        )
        for j in range(ny // LANES):
            grid[j, pl.ds(grid_at, rows), :] = placed[:, j * LANES : (j + 1) * LANES]
        return carry


    def tiles(first, planes):
        return pl.ds(lax.div(first, HALF), planes // HALF)

    def block_copy(k, first, planes, c, d, arrived):
        return pltpu.make_async_remote_copy(
            src_ref=send.at[k, c, d, tiles(first, planes)],
            dst_ref=recv.at[k, c, me_s, tiles(first, planes)],
            send_sem=send_sem.at[k],
            recv_sem=arrived,
            device_id={"slab": d},
            device_id_type=MESH,
        )

    def all_of(k, c, planes, arrived):
        return pltpu.make_async_remote_copy(
            src_ref=recv.at[k, c, pl.ds(0, slab - 1), planes],
            dst_ref=recv.at[k, c, pl.ds(0, slab - 1), planes],
            send_sem=send_sem.at[k],
            recv_sem=arrived,
            device_id={"slab": lax.rem(me_s + 1, slab)},
            device_id_type=MESH,
        )

    def all_sent(k):
        return pltpu.make_async_remote_copy(
            src_ref=send.at[k, :, pl.ds(0, slab - 1)],
            dst_ref=recv.at[k, :, pl.ds(0, slab - 1)],
            send_sem=send_sem.at[k],
            recv_sem=recv_sem.at[k, 0],
            device_id={"slab": lax.rem(me_s + 1, slab)},
            device_id_type=MESH,
        )

    def own_copy(k, c):
        return pltpu.make_async_copy(send.at[k, c, me_s], recv.at[k, c, me_s], own_sem.at[k, c])

    lane = lax.broadcasted_iota(jnp.int32, (ROWS, LANES), 1)

    def rows_pass(k, c, first, planes):
        lefts = []
        for i in range(slab):
            pieces = []
            for part in range(2):
                at = (part * coils + c) * slab + i
                for j in range(ny // LANES):
                    pieces.append(grid[j, pl.ds(first * rows + at, planes, stride=rows), :])
            lefts.append(jnp.concatenate(pieces, axis=1))
        hybrid = jnp.dot(
            jnp.concatenate(lefts, axis=0).astype(jnp.bfloat16),
            ky_tab[...],
            preferred_element_type=jnp.float32,
        )
        turned = []
        for part in range(2):
            values = []
            for i in range(slab):
                value = hybrid[i * planes : (i + 1) * planes, part * ny : (part + 1) * ny]
                values.append(pltpu.roll(value, i * yb, 1) if i else value)
            turned.append(values)
        for d in range(slab):
            for j in range(ny // LANES):
                low, high = j * LANES // yb, ((j + 1) * LANES - 1) // yb
                cut = slice(j * LANES, (j + 1) * LANES)
                parts = []
                for values in turned:
                    tile = values[(low - d) % slab][:, cut]
                    for p in range(low + 1, high + 1):
                        tile = jnp.where(
                            lane[:planes] >= p * yb - j * LANES, values[(p - d) % slab][:, cut], tile
                        )
                    parts.append(tile)
                for g in range(planes // HALF):
                    both = [tile[g * HALF : (g + 1) * HALF] for tile in parts]
                    send[k, c, d, lax.div(first, HALF) + g, :, cut] = jnp.concatenate(
                        both, axis=0
                    ).astype(jnp.bfloat16)

    def send_rows(k, c, first, planes):
        for d in across(me_s, slab) + beside(me_s, slab):
            block_copy(k, first, planes, c, d, recv_sem.at[k, c]).start()

    def fill(k, b):
        load_k(k, b).wait()
        lax.fori_loop(0, slab, functools.partial(unpack, chunk_of(k) * slab, b), 0)

    def later_loads():
        for j in range(blocks, chunks * blocks):
            load_k(jnp.int32(j // blocks), j % blocks).start()
        load_m.start()
        load_z.start()

    def block_pass(j, carry):
        k, b = lax.div(j, blocks), lax.rem(j, blocks)
        first = pl.multiple_of(b * ROWS, ROWS)
        fill(k, b)
        lax.fori_loop(0, count, functools.partial(place, first), 0, unroll=UNROLL)
        if not split:

            @pl.when(j == 0)
            def _():
                load_y.wait()

        def one_coil(c, inner):
            rows_pass(k, c, first, ROWS)

            @pl.when((k == 0) & (last > 0))
            def _():
                send_rows(k, c, first, ROWS)

            @pl.when(b == blocks - 1)
            def _():
                own_copy(k, c).start()

            return inner

        if not split:

            @pl.when(j == 0)
            def _():
                pl.semaphore_wait(barrier, slab + coil - 2)
                later_loads()

        lax.fori_loop(0, coils, one_coil, 0)

        @pl.when((k > 0) & (k < last) & (b == blocks - 1))
        def _():
            for d in across(me_s, slab) + beside(me_s, slab):
                for c in range(coils):
                    block_copy(k, 0, kzp, c, d, recv_sem.at[k, c]).start()

        return carry

    def half_pass(q, carry):
        first = pl.multiple_of(lax.div(q, coils) * HALF, HALF)
        c = lax.rem(q, coils)

        @pl.when(c == 0)
        def _():
            lax.fori_loop(0, HALF, functools.partial(place, first), 0, unroll=HALF)

        @pl.when(q == 0)
        def _():
            load_y.wait()

        rows_pass(0, c, first, HALF)

        @pl.when(q == 0)
        def _():
            pl.semaphore_wait(barrier, slab + coil - 2)

        send_rows(0, c, first, HALF)
        return carry

    load_i.wait()
    if split:
        fill(jnp.int32(0), 0)
        lax.fori_loop(0, coils * (ROWS // HALF), half_pass, 0)
        later_loads()
        if blocks == 1:
            for c in range(coils):
                own_copy(0, c).start()
    lax.fori_loop(int(split), chunks * blocks, block_pass, 0)
    far, near = across(me_s, slab), beside(me_s, slab)
    middle = len(far) // 2

    def send_early(d):
        for c in range(coils):
            if early:
                block_copy(last, 0, early, c, d, recv_sem.at[last, c]).start()

    def send_last(d):
        for c in range(coils):
            block_copy(last, early, ROWS, c, d, last_sem.at[c]).start()

    for d in far[:middle] + near:
        send_early(d)
        send_last(d)
    for d in far[middle:]:
        send_early(d)
    for d in far[middle:]:
        send_last(d)
    load_m.wait()
    load_z.wait()

    def part_copy(k, q):
        owner = chunk_of(k) * owners + q
        return pltpu.make_async_remote_copy(
            src_ref=part_send.at[chunk_of(k), pl.ds(q * xo, xo)],
            dst_ref=part_recv.at[lax.rem(owner - me_c + coil, coil)],
            send_sem=psend_sem.at[k, q],
            recv_sem=precv_sem.at[lax.rem(owner - me_c + coil, coil)],
            device_id={"coil": owner},
            device_id_type=MESH,
        )

    def depth(k, c, at, planes):
        block = recv[k, c, :, tiles(at, planes)].reshape(slab * 2 * planes, slab * yb)
        table = kz_tab[:, tiles(at, planes)].reshape(slab * 2 * planes, 2 * nz)
        return lax.dot_general(
            block, table, (((0,), (0,)), ((), ())), preferred_element_type=jnp.float32
        )

    def combined(c, p, x):
        real = image[c, pl.ds(p * yb, yb), :nz]
        imag = image[c, pl.ds(p * yb, yb), nz:]
        map_real = maps[0, c, x].astype(jnp.float32)
        map_imag = maps[1, c, x].astype(jnp.float32)
        return map_real * real + map_imag * imag, map_real * imag - map_imag * real

    def depth_pass(k, carry):
        first = chunk_of(k) * slab

        def one_coil(c, inner):
            own_copy(k, c).wait()
            @pl.when(k < last)
            def _():
                all_of(k, c, tiles(0, kzp), recv_sem.at[k, c]).wait_recv()

            image[c] = depth(k, c, 0, kzp)
            return inner

        lax.fori_loop(0, coils, one_coil, 0)
        for p in range(slab):
            x = lax.rem(p - me_s + slab, slab)
            add_real, add_imag = combined(0, p, first + x)
            for c in range(1, coils):
                term_real, term_imag = combined(c, p, first + x)
                add_real, add_imag = add_real + term_real, add_imag + term_imag
            part_send[chunk_of(k), x, 0] = add_real.astype(jnp.bfloat16)
            part_send[chunk_of(k), x, 1] = add_imag.astype(jnp.bfloat16)
        for q in range(owners):
            @pl.when(chunk_of(k) * owners + q != me_c)
            def _():
                part_copy(k, q).start()
        return carry

    def wait_parts():
        for o in range(1, coil):
            pltpu.make_async_remote_copy(
                src_ref=part_recv.at[o],
                dst_ref=part_recv.at[o],
                send_sem=psend_sem.at[0, 0],
                recv_sem=precv_sem.at[o],
                device_id={"coil": lax.rem(me_c + o, coil)},
                device_id_type=MESH,
            ).wait_recv()

    def drain(k, carry):
        all_sent(k).wait_send()
        for q in range(owners):
            @pl.when(chunk_of(k) * owners + q != me_c)
            def _():
                part_copy(k, q).wait_send()
        return carry

    own_chunk = lax.div(me_c, owners)

    if owners == 1 and coil > 1:
        lax.fori_loop(0, last, depth_pass, 0)
        wait_parts()

        def add_up(c):
            for p in range(slab):
                x = lax.rem(p - me_s + slab, slab)
                add_real, add_imag = combined(c, p, own_chunk * slab + x)
                out_ref[x, 0] += add_real
                out_ref[x, 1] += add_imag

        def total(i, carry):
            value = part_recv[1, i].astype(jnp.float32)
            for o in range(2, coil):
                value = value + part_recv[o, i].astype(jnp.float32)
            out_ref[i] = value
            return carry

        lax.fori_loop(0, xo, total, 0)
        for c in range(coils):
            own_copy(last, c).wait()
        if blocks > 1:
            for c in range(coils):
                all_of(last, c, tiles(0, early), recv_sem.at[last, c]).wait_recv()
                image[c] = depth(last, c, 0, early)
            for c in range(coils):
                add_up(c)
        lax.fori_loop(0, last, drain, 0)
        final = coils - 1
        for p in range(slab):
            x = own_chunk * slab + lax.rem(p - me_s + slab, slab)
            for part in range(2):
                held_maps[part, p] = maps[part, final, x]
        held_table[...] = kz_tab[:, tiles(early, ROWS)]
        for c in range(final):
            all_of(last, c, tiles(early, ROWS), last_sem.at[c]).wait_recv()
            image[c] = depth(last, c, early, ROWS)
            add_up(c)
        all_of(last, final, tiles(early, ROWS), last_sem.at[final]).wait_recv()
        block_ref[...] = recv[last, final, :, tiles(early, ROWS)]
        drain(last, 0)
    else:

        lax.fori_loop(0, last, depth_pass, 0)
        for c in range(coils):
            if blocks > 1:
                all_of(last, c, tiles(0, early), recv_sem.at[last, c]).wait_recv()
            all_of(last, c, tiles(early, ROWS), last_sem.at[c]).wait_recv()
        depth_pass(last, 0)
        wait_parts()
        own_at = lax.rem(me_c, owners) * xo

        def total(i, carry):
            value = part_send[own_chunk, own_at + i].astype(jnp.float32)
            for o in range(1, coil):
                value = value + part_recv[o, i].astype(jnp.float32)
            out_ref[i] = value
            return carry

        lax.fori_loop(0, xo, total, 0)
        lax.fori_loop(0, chunks, drain, 0)
        for unused in (block_ref, held_maps, held_table):
            unused[...] = jnp.zeros_like(unused)


def finish(slab, out_ref_in, block_ref, held_maps, held_table, out_ref, image, stage, sem):
    me_s = lax.axis_index("slab")
    yb, nz = stage.shape[2:]
    ny = slab * yb
    depth = block_ref.shape[0] * block_ref.shape[1] * block_ref.shape[2]
    table = held_table[...].reshape(depth, 2 * nz)
    image[...] = lax.dot_general(
        block_ref[...].reshape(depth, ny),
        table,
        (((0,), (0,)), ((), ())),
        preferred_element_type=jnp.float32,
    )
    copies = []
    for p in range(slab):
        x = lax.rem(p - me_s + slab, slab)
        real = image[p * yb : (p + 1) * yb, :nz]
        imag = image[p * yb : (p + 1) * yb, nz:]
        map_real = held_maps[0, p].astype(jnp.float32)
        map_imag = held_maps[1, p].astype(jnp.float32)
        stage[p, 0] = out_ref_in[x, 0] + (map_real * real + map_imag * imag)
        stage[p, 1] = out_ref_in[x, 1] + (map_real * imag - map_imag * real)
        copies.append(pltpu.make_async_copy(stage.at[p], out_ref.at[x], sem.at[p]))
        copies[-1].start()
    for copy in copies:
        copy.wait()


def local(mesh, kspace, coil_maps, line_index):
    slab, coil = mesh.shape["slab"], mesh.shape["coil"]
    _, coils, offs, xr, kzb, lines = kspace.shape
    yb, nz = coil_maps.shape[3:]
    ny = yb * slab
    kzp = up(kzb, 16)
    dims = (slab, coil, coils, offs, xr, kzb, kzp, lines, ny, yb, nz)
    chunks, xo = xr // slab, xr // coil
    owners = slab // xo
    rows = 2 * coils * slab
    f32, bf16 = jnp.float32, jnp.bfloat16

    ky_table = np.concatenate(dense_table(np.arange(ny), np.ones(ny), ny), 0)
    local_kz = np.arange(kzp)
    per_slab = []
    for s in range(slab):
        per_slab += dense_table(s * kzb + local_kz, (local_kz < kzb) * 1.0, nz)
    kz_table = np.concatenate(per_slab, 0).reshape(slab, 2, kzp // HALF, HALF, 2 * nz)
    kz_table = kz_table.swapaxes(1, 2).reshape(slab, kzp // HALF, 2 * HALF, 2 * nz)
    ky_table = jnp.asarray(ky_table.astype(np.float32)).astype(bf16)
    kz_table = jnp.asarray(kz_table.astype(np.float32)).astype(bf16)

    vmem, hbm = pl.BlockSpec(memory_space=pltpu.VMEM), pl.BlockSpec(memory_space=pltpu.HBM)
    dma = pltpu.SemaphoreType.DMA
    direct = owners == 1 and coil > 1
    small = (lambda *shape: shape) if direct else (lambda *shape: (8, 128))
    result = pl.pallas_call(
        functools.partial(kernel, dims),
        out_shape=[
            jax.ShapeDtypeStruct((xo, 2, yb, nz), f32),
            jax.ShapeDtypeStruct(small(slab, ROWS // HALF, 2 * HALF, ny), bf16),
            jax.ShapeDtypeStruct(small(2, slab, yb, nz), bf16),
            jax.ShapeDtypeStruct(small(slab, ROWS // HALF, 2 * HALF, 2 * nz), bf16),
        ],
        in_specs=[hbm] * 5,
        out_specs=[vmem] * 4,
        scratch_shapes=[
            pltpu.VMEM(kspace.shape, bf16),
            pltpu.VMEM(line_index.shape, jnp.int32),
            pltpu.VMEM((offs, rows * up(kzb, 8), lines), f32),
            pltpu.VMEM((ny // LANES, kzp * rows, LANES), f32),
            pltpu.VMEM(coil_maps.shape, bf16),
            pltpu.VMEM(ky_table.shape, bf16),
            pltpu.VMEM(kz_table.shape, bf16),
            pltpu.VMEM((chunks, coils, slab, kzp // HALF, 2 * HALF, ny), bf16),
            pltpu.VMEM((chunks, coils, slab, kzp // HALF, 2 * HALF, ny), bf16),
            pltpu.VMEM((coils, ny, 2 * nz), f32),
            pltpu.VMEM((chunks, slab, 2, yb, nz), bf16),
            pltpu.VMEM((coil, xo, 2, yb, nz), bf16),
            dma((4,)),
            dma((chunks, kzp // ROWS)),
            dma((chunks,)),
            dma((chunks, coils)),
            dma((coils,)),
            dma((chunks, coils)),
            dma((chunks, owners)),
            dma((coil,)),
        ],
        compiler_params=pltpu.CompilerParams(
            collective_id=0, has_side_effects=True, vmem_limit_bytes=VLIM * 1024 * 1024
        ),
    )(
        *(
            pltpu.with_memory_space_constraint(operand, pltpu.HBM)
            for operand in (kspace, coil_maps, line_index, ky_table, kz_table)
        )
    )
    if not direct:
        return result[0]
    return pl.pallas_call(
        functools.partial(finish, slab),
        out_shape=jax.ShapeDtypeStruct((xo, 2, yb, nz), f32),
        in_specs=[vmem] * 4,
        out_specs=hbm,
        scratch_shapes=[
            pltpu.VMEM((ny, 2 * nz), f32),
            pltpu.VMEM((xo, 2, yb, nz), f32),
            dma((xo,)),
        ],
        compiler_params=pltpu.CompilerParams(vmem_limit_bytes=FINISH * 1024 * 1024),
    )(*result)


def solution(mesh):
    placed = (
        P(None, "coil", None, None, "slab", None),
        P(None, "coil", None, "slab", None),
        P(None, "slab", None),
    )
    return jax.shard_map(
        functools.partial(local, mesh),
        mesh=mesh,
        in_specs=placed,
        out_specs=P("coil", None, "slab", None),
        check_vma=False,
    )
```

```python
import functools
import math

import jax
import jax.numpy as jnp
import numpy as np
from jax import lax
from jax.experimental import pallas as pl
from jax.experimental.pallas import tpu as pltpu
from jax.sharding import PartitionSpec as P

PHASES = 8
LANES = 128
UNROLL = 16
VLIM = 48
FINISH = 8
ROWS = 16
HALF = 8
MESH = pl.DeviceIdType.MESH


def across(me, slab):
    half = slab // 2
    other = half - lax.div(me, half) * half
    return [other + i for i in range(half)]


def beside(me, slab):
    half = slab // 2
    first = lax.div(me, half) * half
    return [first + lax.rem(me + i, half) for i in range(1, half)]


def up(value, unit):
    return -(-value // unit) * unit


def dense_table(rows, row_ok, length):
    turns = rows[:, None].astype(np.int64) * np.arange(length)[None, :] % length
    angles = turns.astype(np.float64) * (2.0 * math.pi / length)
    scaling = row_ok[:, None] / math.sqrt(length)
    cos, sin = np.cos(angles) * scaling, np.sin(angles) * scaling
    return np.concatenate([cos, sin], 1), np.concatenate([-sin, cos], 1)


def kernel(
    dims,
    kspace_ref, maps_ref, index_ref, ky_ref, kz_ref, out_ref, block_ref, held_maps, held_table,
    raw, index, samples, grid, maps, ky_tab, kz_tab, send, recv, image, part_send, part_recv,
    in_sem, load_sem, send_sem, recv_sem, last_sem, own_sem, psend_sem, precv_sem,
):
    slab, coil, coils, offs, xr, kzb, kzp, lines, ny, yb, nz = dims
    me_s, me_c = lax.axis_index("slab"), lax.axis_index("coil")
    rows = 2 * coils * slab
    kzs = up(kzb, 8)
    chunks = xr // slab
    last = chunks - 1
    xo = xr // coil
    owners = slab // xo
    blocks = kzp // ROWS
    early = (blocks - 1) * ROWS
    split = last > 0 and kzb % ROWS == 0

    barrier = pltpu.get_barrier_semaphore()
    for d in across(me_s, slab) + beside(me_s, slab):
        pl.semaphore_signal(barrier, inc=1, device_id={"slab": d}, device_id_type=MESH)
    for o in range(1, coil):
        pl.semaphore_signal(
            barrier, inc=1, device_id={"coil": lax.rem(me_c + o, coil)}, device_id_type=MESH
        )

    def chunk_of(k):
        own = lax.div(me_c, owners)
        if chunks % 2:
            return lax.rem(own + 1 + k, chunks)
        pair = lax.rem(lax.div(own, 2) + 1 + lax.div(k, 2), chunks // 2)
        return 2 * pair + lax.rem(own + 1 + k, 2)

    count = min(ROWS, kzb)

    def load_k(k, b):
        at = pl.ds(chunk_of(k) * slab, slab)
        planes = pl.ds(b * ROWS, count)
        return pltpu.make_async_copy(
            kspace_ref.at[:, :, :, at, planes], raw.at[:, :, :, at, planes], load_sem.at[k, b]
        )

    load_i = pltpu.make_async_copy(index_ref, index, in_sem.at[3])
    load_m = pltpu.make_async_copy(maps_ref, maps, in_sem.at[0])
    load_y = pltpu.make_async_copy(ky_ref, ky_tab, in_sem.at[1])
    load_z = pltpu.make_async_copy(kz_ref, kz_tab, in_sem.at[2])
    load_k(jnp.int32(0), 0).start()
    load_i.start()
    load_y.start()
    for b in range(1, blocks):
        load_k(jnp.int32(0), b).start()

    if kzp != kzb:
        grid[...] = jnp.zeros_like(grid)

    def unpack(first, b, i, carry):
        kz_at = pl.multiple_of(b * ROWS, ROWS)
        for c in range(coils):
            for t in range(offs):
                angle = 2.0 * math.pi * t / PHASES
                real = raw[0, c, t, first + i, pl.ds(kz_at, count)].astype(jnp.float32)
                imag = raw[1, c, t, first + i, pl.ds(kz_at, count)].astype(jnp.float32)
                if t:
                    cosine, sine = math.cos(angle), math.sin(angle)
                    real, imag = cosine * real + sine * imag, cosine * imag - sine * real
                for part, value in ((0, real), (1, imag)):
                    at = pl.multiple_of(((part * coils + c) * slab + i) * kzs + kz_at, 8)
                    samples[t, pl.ds(at, count), :] = value
        return carry

    ky_at = lax.broadcasted_iota(jnp.int32, (ny, offs * lines), 0)

    def place(first_kz, step, carry):
        kz = first_kz + step
        picked = jnp.concatenate([index[t, pl.ds(kz, 1), :] for t in range(offs)], axis=1)
        hot = jnp.where(ky_at == picked, 1.0, 0.0).astype(jnp.bfloat16)
        left = jnp.concatenate(
            [samples[t, pl.ds(kz, rows, stride=kzs), :].astype(jnp.bfloat16) for t in range(offs)],
            axis=1,
        )
        grid_at = pl.multiple_of(kz * rows, 8)
        placed = lax.dot_general(
            left, hot, (((1,), (1,)), ((), ())), preferred_element_type=jnp.float32
        )
        for j in range(ny // LANES):
            grid[j, pl.ds(grid_at, rows), :] = placed[:, j * LANES : (j + 1) * LANES]
        return carry


    def tiles(first, planes):
        return pl.ds(lax.div(first, HALF), planes // HALF)

    def block_copy(k, first, planes, c, d, arrived):
        return pltpu.make_async_remote_copy(
            src_ref=send.at[k, c, d, tiles(first, planes)],
            dst_ref=recv.at[k, c, me_s, tiles(first, planes)],
            send_sem=send_sem.at[k],
            recv_sem=arrived,
            device_id={"slab": d},
            device_id_type=MESH,
        )

    def all_of(k, c, planes, arrived):
        return pltpu.make_async_remote_copy(
            src_ref=recv.at[k, c, pl.ds(0, slab - 1), planes],
            dst_ref=recv.at[k, c, pl.ds(0, slab - 1), planes],
            send_sem=send_sem.at[k],
            recv_sem=arrived,
            device_id={"slab": lax.rem(me_s + 1, slab)},
            device_id_type=MESH,
        )

    def all_sent(k):
        return pltpu.make_async_remote_copy(
            src_ref=send.at[k, :, pl.ds(0, slab - 1)],
            dst_ref=recv.at[k, :, pl.ds(0, slab - 1)],
            send_sem=send_sem.at[k],
            recv_sem=recv_sem.at[k, 0],
            device_id={"slab": lax.rem(me_s + 1, slab)},
            device_id_type=MESH,
        )

    def own_copy(k, c):
        return pltpu.make_async_copy(send.at[k, c, me_s], recv.at[k, c, me_s], own_sem.at[k, c])

    lane = lax.broadcasted_iota(jnp.int32, (ROWS, LANES), 1)

    def rows_pass(k, c, first, planes):
        lefts = []
        for i in range(slab):
            pieces = []
            for part in range(2):
                at = (part * coils + c) * slab + i
                for j in range(ny // LANES):
                    pieces.append(grid[j, pl.ds(first * rows + at, planes, stride=rows), :])
            lefts.append(jnp.concatenate(pieces, axis=1))
        hybrid = jnp.dot(
            jnp.concatenate(lefts, axis=0).astype(jnp.bfloat16),
            ky_tab[...],
            preferred_element_type=jnp.float32,
        )
        turned = []
        for part in range(2):
            values = []
            for i in range(slab):
                value = hybrid[i * planes : (i + 1) * planes, part * ny : (part + 1) * ny]
                values.append(pltpu.roll(value, i * yb, 1) if i else value)
            turned.append(values)
        for d in range(slab):
            for j in range(ny // LANES):
                low, high = j * LANES // yb, ((j + 1) * LANES - 1) // yb
                cut = slice(j * LANES, (j + 1) * LANES)
                parts = []
                for values in turned:
                    tile = values[(low - d) % slab][:, cut]
                    for p in range(low + 1, high + 1):
                        tile = jnp.where(
                            lane[:planes] >= p * yb - j * LANES, values[(p - d) % slab][:, cut], tile
                        )
                    parts.append(tile)
                for g in range(planes // HALF):
                    both = [tile[g * HALF : (g + 1) * HALF] for tile in parts]
                    send[k, c, d, lax.div(first, HALF) + g, :, cut] = jnp.concatenate(
                        both, axis=0
                    ).astype(jnp.bfloat16)

    def send_rows(k, c, first, planes):
        for d in across(me_s, slab) + beside(me_s, slab):
            block_copy(k, first, planes, c, d, recv_sem.at[k, c]).start()

    def fill(k, b):
        load_k(k, b).wait()
        lax.fori_loop(0, slab, functools.partial(unpack, chunk_of(k) * slab, b), 0)

    def later_loads():
        for j in range(blocks, chunks * blocks):
            load_k(jnp.int32(j // blocks), j % blocks).start()
        load_m.start()
        load_z.start()

    def block_pass(j, carry):
        k, b = lax.div(j, blocks), lax.rem(j, blocks)
        first = pl.multiple_of(b * ROWS, ROWS)
        fill(k, b)
        lax.fori_loop(0, count, functools.partial(place, first), 0, unroll=UNROLL)
        if not split:

            @pl.when(j == 0)
            def _():
                load_y.wait()

        def one_coil(c, inner):
            rows_pass(k, c, first, ROWS)

            @pl.when((k == 0) & (last > 0))
            def _():
                send_rows(k, c, first, ROWS)

            @pl.when(b == blocks - 1)
            def _():
                own_copy(k, c).start()

            return inner

        if not split:

            @pl.when(j == 0)
            def _():
                pl.semaphore_wait(barrier, slab + coil - 2)
                later_loads()

        lax.fori_loop(0, coils, one_coil, 0)

        @pl.when((k > 0) & (k < last) & (b == blocks - 1))
        def _():
            for d in across(me_s, slab) + beside(me_s, slab):
                for c in range(coils):
                    block_copy(k, 0, kzp, c, d, recv_sem.at[k, c]).start()

        return carry

    def half_pass(q, carry):
        first = pl.multiple_of(lax.div(q, coils) * HALF, HALF)
        c = lax.rem(q, coils)

        @pl.when(c == 0)
        def _():
            lax.fori_loop(0, HALF, functools.partial(place, first), 0, unroll=HALF)

        @pl.when(q == 0)
        def _():
            load_y.wait()

        rows_pass(0, c, first, HALF)

        @pl.when(q == 0)
        def _():
            pl.semaphore_wait(barrier, slab + coil - 2)

        send_rows(0, c, first, HALF)
        return carry

    load_i.wait()
    if split:
        fill(jnp.int32(0), 0)
        lax.fori_loop(0, coils * (ROWS // HALF), half_pass, 0)
        later_loads()
        if blocks == 1:
            for c in range(coils):
                own_copy(0, c).start()
    lax.fori_loop(int(split), chunks * blocks, block_pass, 0)
    far, near = across(me_s, slab), beside(me_s, slab)
    middle = len(far) // 2

    def send_early(d):
        for c in range(coils):
            if early:
                block_copy(last, 0, early, c, d, recv_sem.at[last, c]).start()

    def send_last(d):
        for c in range(coils):
            block_copy(last, early, ROWS, c, d, last_sem.at[c]).start()

    for d in far[:middle] + near:
        send_early(d)
        send_last(d)
    for d in far[middle:]:
        send_early(d)
    for d in far[middle:]:
        send_last(d)
    load_m.wait()
    load_z.wait()

    def part_copy(k, q):
        owner = chunk_of(k) * owners + q
        return pltpu.make_async_remote_copy(
            src_ref=part_send.at[chunk_of(k), pl.ds(q * xo, xo)],
            dst_ref=part_recv.at[lax.rem(owner - me_c + coil, coil)],
            send_sem=psend_sem.at[k, q],
            recv_sem=precv_sem.at[lax.rem(owner - me_c + coil, coil)],
            device_id={"coil": owner},
            device_id_type=MESH,
        )

    def depth(k, c, at, planes):
        block = recv[k, c, :, tiles(at, planes)].reshape(slab * 2 * planes, slab * yb)
        table = kz_tab[:, tiles(at, planes)].reshape(slab * 2 * planes, 2 * nz)
        return lax.dot_general(
            block, table, (((0,), (0,)), ((), ())), preferred_element_type=jnp.float32
        )

    def combined(c, p, x):
        real = image[c, pl.ds(p * yb, yb), :nz]
        imag = image[c, pl.ds(p * yb, yb), nz:]
        map_real = maps[0, c, x].astype(jnp.float32)
        map_imag = maps[1, c, x].astype(jnp.float32)
        return map_real * real + map_imag * imag, map_real * imag - map_imag * real

    def depth_pass(k, carry):
        first = chunk_of(k) * slab

        def one_coil(c, inner):
            own_copy(k, c).wait()
            @pl.when(k < last)
            def _():
                all_of(k, c, tiles(0, kzp), recv_sem.at[k, c]).wait_recv()

            image[c] = depth(k, c, 0, kzp)
            return inner

        lax.fori_loop(0, coils, one_coil, 0)
        for p in range(slab):
            x = lax.rem(p - me_s + slab, slab)
            add_real, add_imag = combined(0, p, first + x)
            for c in range(1, coils):
                term_real, term_imag = combined(c, p, first + x)
                add_real, add_imag = add_real + term_real, add_imag + term_imag
            part_send[chunk_of(k), x, 0] = add_real.astype(jnp.bfloat16)
            part_send[chunk_of(k), x, 1] = add_imag.astype(jnp.bfloat16)
        for q in range(owners):
            @pl.when(chunk_of(k) * owners + q != me_c)
            def _():
                part_copy(k, q).start()
        return carry

    def wait_parts():
        for o in range(1, coil):
            pltpu.make_async_remote_copy(
                src_ref=part_recv.at[o],
                dst_ref=part_recv.at[o],
                send_sem=psend_sem.at[0, 0],
                recv_sem=precv_sem.at[o],
                device_id={"coil": lax.rem(me_c + o, coil)},
                device_id_type=MESH,
            ).wait_recv()

    def drain(k, carry):
        all_sent(k).wait_send()
        for q in range(owners):
            @pl.when(chunk_of(k) * owners + q != me_c)
            def _():
                part_copy(k, q).wait_send()
        return carry

    own_chunk = lax.div(me_c, owners)

    if owners == 1 and coil > 1:
        lax.fori_loop(0, last, depth_pass, 0)
        wait_parts()

        def add_up(c):
            for p in range(slab):
                x = lax.rem(p - me_s + slab, slab)
                add_real, add_imag = combined(c, p, own_chunk * slab + x)
                out_ref[x, 0] += add_real
                out_ref[x, 1] += add_imag

        def total(i, carry):
            value = part_recv[1, i].astype(jnp.float32)
            for o in range(2, coil):
                value = value + part_recv[o, i].astype(jnp.float32)
            out_ref[i] = value
            return carry

        lax.fori_loop(0, xo, total, 0)
        for c in range(coils):
            own_copy(last, c).wait()
        if blocks > 1:
            for c in range(coils):
                all_of(last, c, tiles(0, early), recv_sem.at[last, c]).wait_recv()
                image[c] = depth(last, c, 0, early)
            for c in range(coils):
                add_up(c)
        lax.fori_loop(0, last, drain, 0)
        final = coils - 1
        for p in range(slab):
            x = own_chunk * slab + lax.rem(p - me_s + slab, slab)
            for part in range(2):
                held_maps[part, p] = maps[part, final, x]
        held_table[...] = kz_tab[:, tiles(early, ROWS)]
        for c in range(final):
            all_of(last, c, tiles(early, ROWS), last_sem.at[c]).wait_recv()
            image[c] = depth(last, c, early, ROWS)
            add_up(c)
        all_of(last, final, tiles(early, ROWS), last_sem.at[final]).wait_recv()
        block_ref[...] = recv[last, final, :, tiles(early, ROWS)]
        drain(last, 0)
    else:

        lax.fori_loop(0, last, depth_pass, 0)
        for c in range(coils):
            if blocks > 1:
                all_of(last, c, tiles(0, early), recv_sem.at[last, c]).wait_recv()
            all_of(last, c, tiles(early, ROWS), last_sem.at[c]).wait_recv()
        depth_pass(last, 0)
        wait_parts()
        own_at = lax.rem(me_c, owners) * xo

        def total(i, carry):
            value = part_send[own_chunk, own_at + i].astype(jnp.float32)
            for o in range(1, coil):
                value = value + part_recv[o, i].astype(jnp.float32)
            out_ref[i] = value
            return carry

        lax.fori_loop(0, xo, total, 0)
        lax.fori_loop(0, chunks, drain, 0)
        for unused in (block_ref, held_maps, held_table):
            unused[...] = jnp.zeros_like(unused)


def finish(slab, out_ref_in, block_ref, held_maps, held_table, out_ref, image, stage, sem):
    me_s = lax.axis_index("slab")
    yb, nz = stage.shape[2:]
    ny = slab * yb
    depth = block_ref.shape[0] * block_ref.shape[1] * block_ref.shape[2]
    table = held_table[...].reshape(depth, 2 * nz)
    copies = []
    cuts = [0, 2 * LANES, ny] if ny > 2 * LANES else [0, ny]
    for low, high in zip(cuts[:-1], cuts[1:], strict=True):
        image[low:high] = lax.dot_general(
            block_ref[:, :, :, low:high].reshape(depth, high - low),
            table,
            (((0,), (0,)), ((), ())),
            preferred_element_type=jnp.float32,
        )
        for p in range(low // yb, high // yb):
            x = lax.rem(p - me_s + slab, slab)
            real = image[p * yb : (p + 1) * yb, :nz]
            imag = image[p * yb : (p + 1) * yb, nz:]
            map_real = held_maps[0, p].astype(jnp.float32)
            map_imag = held_maps[1, p].astype(jnp.float32)
            stage[p, 0] = out_ref_in[x, 0] + (map_real * real + map_imag * imag)
            stage[p, 1] = out_ref_in[x, 1] + (map_real * imag - map_imag * real)
            copies.append(pltpu.make_async_copy(stage.at[p], out_ref.at[x], sem.at[p]))
            copies[-1].start()
    for copy in copies:
        copy.wait()


def local(mesh, kspace, coil_maps, line_index):
    slab, coil = mesh.shape["slab"], mesh.shape["coil"]
    _, coils, offs, xr, kzb, lines = kspace.shape
    yb, nz = coil_maps.shape[3:]
    ny = yb * slab
    kzp = up(kzb, 16)
    dims = (slab, coil, coils, offs, xr, kzb, kzp, lines, ny, yb, nz)
    chunks, xo = xr // slab, xr // coil
    owners = slab // xo
    rows = 2 * coils * slab
    f32, bf16 = jnp.float32, jnp.bfloat16

    ky_table = np.concatenate(dense_table(np.arange(ny), np.ones(ny), ny), 0)
    local_kz = np.arange(kzp)
    per_slab = []
    for s in range(slab):
        per_slab += dense_table(s * kzb + local_kz, (local_kz < kzb) * 1.0, nz)
    kz_table = np.concatenate(per_slab, 0).reshape(slab, 2, kzp // HALF, HALF, 2 * nz)
    kz_table = kz_table.swapaxes(1, 2).reshape(slab, kzp // HALF, 2 * HALF, 2 * nz)
    ky_table = jnp.asarray(ky_table.astype(np.float32)).astype(bf16)
    kz_table = jnp.asarray(kz_table.astype(np.float32)).astype(bf16)

    vmem, hbm = pl.BlockSpec(memory_space=pltpu.VMEM), pl.BlockSpec(memory_space=pltpu.HBM)
    dma = pltpu.SemaphoreType.DMA
    direct = owners == 1 and coil > 1
    small = (lambda *shape: shape) if direct else (lambda *shape: (8, 128))
    result = pl.pallas_call(
        functools.partial(kernel, dims),
        out_shape=[
            jax.ShapeDtypeStruct((xo, 2, yb, nz), f32),
            jax.ShapeDtypeStruct(small(slab, ROWS // HALF, 2 * HALF, ny), bf16),
            jax.ShapeDtypeStruct(small(2, slab, yb, nz), bf16),
            jax.ShapeDtypeStruct(small(slab, ROWS // HALF, 2 * HALF, 2 * nz), bf16),
        ],
        in_specs=[hbm] * 5,
        out_specs=[vmem] * 4,
        scratch_shapes=[
            pltpu.VMEM(kspace.shape, bf16),
            pltpu.VMEM(line_index.shape, jnp.int32),
            pltpu.VMEM((offs, rows * up(kzb, 8), lines), f32),
            pltpu.VMEM((ny // LANES, kzp * rows, LANES), f32),
            pltpu.VMEM(coil_maps.shape, bf16),
            pltpu.VMEM(ky_table.shape, bf16),
            pltpu.VMEM(kz_table.shape, bf16),
            pltpu.VMEM((chunks, coils, slab, kzp // HALF, 2 * HALF, ny), bf16),
            pltpu.VMEM((chunks, coils, slab, kzp // HALF, 2 * HALF, ny), bf16),
            pltpu.VMEM((coils, ny, 2 * nz), f32),
            pltpu.VMEM((chunks, slab, 2, yb, nz), bf16),
            pltpu.VMEM((coil, xo, 2, yb, nz), bf16),
            dma((4,)),
            dma((chunks, kzp // ROWS)),
            dma((chunks,)),
            dma((chunks, coils)),
            dma((coils,)),
            dma((chunks, coils)),
            dma((chunks, owners)),
            dma((coil,)),
        ],
        compiler_params=pltpu.CompilerParams(
            collective_id=0, has_side_effects=True, vmem_limit_bytes=VLIM * 1024 * 1024
        ),
    )(
        *(
            pltpu.with_memory_space_constraint(operand, pltpu.HBM)
            for operand in (kspace, coil_maps, line_index, ky_table, kz_table)
        )
    )
    if not direct:
        return result[0]
    return pl.pallas_call(
        functools.partial(finish, slab),
        out_shape=jax.ShapeDtypeStruct((xo, 2, yb, nz), f32),
        in_specs=[vmem] * 4,
        out_specs=hbm,
        scratch_shapes=[
            pltpu.VMEM((ny, 2 * nz), f32),
            pltpu.VMEM((xo, 2, yb, nz), f32),
            dma((xo,)),
        ],
        compiler_params=pltpu.CompilerParams(vmem_limit_bytes=FINISH * 1024 * 1024),
    )(*result)


def solution(mesh):
    placed = (
        P(None, "coil", None, None, "slab", None),
        P(None, "coil", None, "slab", None),
        P(None, "slab", None),
    )
    return jax.shard_map(
        functools.partial(local, mesh),
        mesh=mesh,
        in_specs=placed,
        out_specs=P("coil", None, "slab", None),
        check_vma=False,
    )
```
